512 devices in a mesh: seq: 64 (over z, y_hi, core), tensor: 8 (over x, y_lo).
Axes of the slice: x: 4, y: 8 (y_hi: 4, y_lo: 2; y = y_hi * 2 + y_lo), z: 8, core: 2. Of those that a mesh axis runs over, the one named last changes fastest.
Arguments:
- q_in: float32 [16384, 5120], P('seq', 'tensor'), may hold values from -520 to 520
- k_in: float32 [16384, 5120], P('seq', 'tensor'), may hold values from -520 to 520
- v_in: bfloat16 [16384, 5120], P('seq', 'tensor'), may hold values from -12 to 12
- q_gain: float32 [5120], P('tensor'), may hold values from 0.8 to 2
- k_gain: float32 [5120], P('tensor'), may hold values from 0.8 to 2
- frames: int32 [128], replicated, may hold values from 0 to 11, never falling along the last dimension, each value on 1 to 12 neighbouring positions
- adjacent: int32 [128, 128], P('seq'), may hold values 0 or 1
Outputs:
- attended: float32 [16384, 5120], P('seq', 'tensor')
The draws below stay inside these ranges and needn't reach their ends.
Inputs may be any that keep to these rules, and one draw needn't show every extreme that they name: `frames`: frame numbers never fall from one block to the next, and each frame spans 1 to 12 consecutive blocks.
All inputs are finite; a program needn't handle non-finite values. No bound on the sum of `adjacent` on one device may be relied on, other than what follows from the above.
Results may differ from the reference program's by a relative error of at most 0.012.
The reference program's roundings to bfloat16 on the way (of `q_norm`, `k_norm` and `rounded_weights`) count: a program that leaves them out, or rounds other values in their place, can miss the bound.
Values may be sent and summed in bfloat16 or wider, within the bound.
A program may use at most 128 MiB of HBM per device.

```python
import math
import jax
import jax.numpy as jnp
import numpy as np
from jax import lax

D = 5120
HEAD_DIM = 128
TOK_DEV = 256
BLOCK = 128
FRAME_BLK = 12
BLOCKS_DEV = 2
BLOCKS = 128
TOKENS = 16384
FRAMES = 12
REACH = 12
N_SEQ = 64


def drawn_input(key, role_index):
    own_key = jax.random.fold_in(key, 101 + role_index)
    split_keys = jax.random.split(own_key, 3)
    scale_top = math.log(10.0)
    entries = jnp.clip(jax.random.normal(split_keys[2], (TOKENS, D), jnp.float32), -4.0, 4.0)
    row_scales = jnp.exp(jax.random.uniform(split_keys[0], (TOKENS, 1), jnp.float32, 0.0, scale_top))
    rising = jnp.exp(jnp.arange(D, dtype=jnp.float32) * (math.log(3.0) / (D - 1)))
    col_scales = jnp.exp(jax.random.uniform(split_keys[1], (1, D), jnp.float32, 0.0, math.log(10.0))) * rising[None, :] / 3.0
    shaped = entries * col_scales
    drawn = shaped * row_scales
    return drawn


def draw_q_in(key, part):
    return drawn_input(key, 0)


def draw_k_in(key, part):
    return drawn_input(key, 1)


def place_ends(array, key, low, top_value):
    longest = array.shape.index(max(array.shape))
    spots = []
    for shift in (0, 1):
        where = [jax.random.randint(jax.random.fold_in(key, axis), (), 0, length) for axis, length in enumerate(array.shape)]
        where[longest] = (where[longest] + shift) % array.shape[longest]
        spots.append(tuple(where))
    return array.at[spots[0]].set(low).at[spots[1]].set(top_value)


def levels(key, dims, shards, smallest, high):
    level, own = 1.0, jax.random.fold_in(key, 6)
    for position, blocks in shards:
        draws = jnp.exp(jax.random.uniform(jax.random.fold_in(own, position), (blocks,), jnp.float32, smallest / len(shards), high / len(shards)))
        level = level * jnp.repeat(draws, dims[position] // blocks).reshape([-1 if axis == position else 1 for axis in range(len(dims))])
    return level


def split_up(count, total, limit, lean):
    weights = [(1 << 20) // math.isqrt(rank ** lean) + 1 for rank in range(2, count + 1)]
    spare, counts = total - limit - (count - 1), [1] * (count - 1)
    while spare > 0:
        free = [i for i in range(count - 1) if counts[i] < limit]
        whole, left = sum([weights[i] for i in free]), spare
        for i in free:
            extra = min(limit - counts[i], max(1, left * weights[i] // whole), spare)
            counts[i] = counts[i] + extra
            spare = spare - extra
    return np.array([limit] + counts)


def uneven_parts(key, number_of, total, most, slope):
    if number_of == 2:
        one = jax.random.randint(key, (), max(1, total - most), min(most, total - 1) + 1)
        return jnp.stack([one, total - one])
    lengths = jnp.asarray(split_up(number_of, total, most, slope), jnp.int32)
    pairs = (number_of - 1) // 2
    source_of, taker = lengths[1:1 + 2 * pairs:2], lengths[2:2 + 2 * pairs:2]
    room = jnp.minimum(source_of - 1, most - taker)
    moved = jax.random.randint(jax.random.fold_in(key, 1), (pairs,), 0, 1 << 20) % (room + 1)
    lengths = lengths.at[1:1 + 2 * pairs:2].set(source_of - moved).at[2:2 + 2 * pairs:2].set(taker + moved)
    return lengths[jax.random.permutation(jax.random.fold_in(key, 2), number_of)]


def bell_draw(key, extent, spread, bound, cuts=(), kind=jnp.bfloat16):
    values = jax.random.normal(key, extent, jnp.float32) * spread
    if len(cuts) > 0:
        values = levels(key, extent, cuts, -0.22, 0.18) * values
    return jnp.clip(values, min=-bound, max=bound).astype(kind)


def setup_inputs(seed: int = 0) -> dict:
    key_list = jax.random.split(jax.random.key(seed), 8)
    q_in = draw_q_in(jax.random.fold_in(key_list[7], 71), 0)
    k_in = draw_k_in(jax.random.fold_in(key_list[7], 71), 0)
    v_in = bell_draw(key_list[2], (TOKENS, D), 2.0, 12.0, ((0, 64), (1, 8)))
    q_gain = jnp.clip(0.8 + 1.2 * jax.random.uniform(key_list[3], (D,), jnp.float32) ** levels(key_list[3], (D,), ((0, 8),), -0.2, 0.2), 0.8, 2.0)
    k_gain = jnp.clip(0.8 + 1.2 * jax.random.uniform(key_list[4], (D,), jnp.float32) ** levels(key_list[4], (D,), ((0, 8),), -0.2, 0.2), 0.8, 2.0)
    frames = jnp.searchsorted(jnp.cumsum(uneven_parts(key_list[5], FRAMES, BLOCKS, FRAME_BLK, 0)), jnp.arange(BLOCKS), side="right").astype(jnp.int32)
    adjacent = place_ends((jax.random.randint(key_list[6], (BLOCKS, BLOCKS), 0, 2) < 1).astype(jnp.int32), jax.random.fold_in(key_list[6], 1), 0, 1)
    return {"q_in": q_in, "k_in": k_in, "v_in": v_in, "q_gain": q_gain, "k_gain": k_gain, "frames": frames, "adjacent": adjacent}


epsilon = 1e-06
blocked = -1e+30

def normalized(inputs, gain_row):
    return (inputs / jnp.sqrt(lax.optimization_barrier(jnp.mean(inputs * inputs, axis=1, keepdims=True)) + epsilon) * gain_row).astype(jnp.bfloat16)

def reference(q_in, k_in, v_in, q_gain, k_gain, frames, adjacent):
    q_norm = normalized(q_in, q_gain)
    k_norm = normalized(k_in, k_gain)
    head_count = D // HEAD_DIM
    margin = REACH * TOK_DEV
    window = (2 * REACH + 1) * TOK_DEV
    window_blocks = (2 * REACH + 1) * BLOCKS_DEV
    margin_blocks = REACH * BLOCKS_DEV
    padded_keys = jnp.pad(k_norm, ((margin, margin), (0, 0)))
    padded_values = jnp.pad(v_in, ((margin, margin), (0, 0)))
    padded_frames = jnp.pad(frames, (margin_blocks, margin_blocks), constant_values=-1000)
    padded_adjacent = jnp.pad(adjacent, ((0, 0), (margin_blocks, margin_blocks)))
    score_scale = 1.0 / math.sqrt(HEAD_DIM)

    def one_device(device):
        first_row = (device * TOK_DEV).astype(jnp.int32)
        first_block = (device * BLOCKS_DEV).astype(jnp.int32)
        queries = lax.dynamic_slice_in_dim(q_norm, first_row, TOK_DEV, 0).astype(jnp.float32).reshape(TOK_DEV, head_count, HEAD_DIM)
        key_rows = lax.dynamic_slice_in_dim(padded_keys, first_row, window, 0).astype(jnp.float32).reshape(window, head_count, HEAD_DIM)
        value_rows = lax.dynamic_slice_in_dim(padded_values, first_row, window, 0).astype(jnp.float32).reshape(window, head_count, HEAD_DIM)
        query_frames = lax.dynamic_slice_in_dim(frames, first_block, BLOCKS_DEV, 0)
        key_frames = lax.dynamic_slice_in_dim(padded_frames, first_block, window_blocks, 0)
        adjacent_rows = lax.dynamic_slice(padded_adjacent, (first_block, first_block), (BLOCKS_DEV, window_blocks))
        frame_gap = jnp.abs(query_frames[:, None] - key_frames[None, :])
        allowed = (frame_gap == 0) | (frame_gap == 1) & (adjacent_rows == 1)
        scores = jnp.einsum('thd,uhd->htu', queries, key_rows, precision=lax.Precision.HIGHEST) * score_scale
        tiled_scores = scores.reshape(head_count, BLOCKS_DEV, BLOCK, window_blocks, BLOCK)
        tiled_scores = jnp.where(allowed[None, :, None, :, None], tiled_scores, blocked)
        scores = tiled_scores.reshape(head_count, TOK_DEV, window)
        row_max = lax.optimization_barrier(jnp.max(scores, axis=2, keepdims=True))
        weights = jnp.exp(scores - row_max)
        row_total = lax.optimization_barrier(jnp.sum(weights, axis=2))
        rounded_weights = weights.astype(jnp.bfloat16).astype(jnp.float32)
        mixed_sum = jnp.einsum('htu,uhd->thd', rounded_weights, value_rows, precision=lax.Precision.HIGHEST)
        return (mixed_sum / row_total.T[:, :, None]).reshape(TOK_DEV, D)
    results = lax.map(one_device, jnp.arange(N_SEQ, dtype=jnp.int32))
    return results.reshape(TOKENS, D)
```

```python
import math

import jax
import jax.numpy as jnp
from jax import lax
from jax.experimental import pallas as pl
from jax.experimental.pallas import tpu as pltpu
from jax.sharding import PartitionSpec as P

HD = 128
TOK = 256
HEADS = 5
CHIPS = 4
PLANES = 8
TENSOR = 8
SLOTS = 28
MESH = pl.DeviceIdType.MESH
EPS = 1e-06
BLOCKED = -1e30
EXP2_SCALE = math.log2(math.e) / math.sqrt(HD)


def place():
    s = lax.axis_index("seq")
    return lax.div(s, 8), lax.rem(lax.div(s, 2), 4), lax.rem(s, 2), lax.axis_index("tensor")


def columns(head):
    return pl.ds(pl.multiple_of(head * HD, HD), HD)


def gather_kernel(
    q_ref, k_ref, v_ref, qg_ref, kg_ref, adj_ref,
    kvu, kv4, qu, q4, adju,
    qn, kn, stat, statr, relay,
    ssem, lsem, ru, r4, rq, ra, rrelay, rstat,
):
    z, h, k, t = place()
    other = 1 - k

    def dev(zz, hh, kk):
        return (lax.rem(zz + PLANES, PLANES) * 8 + hh * 2 + kk, t)

    def chip(step):
        return lax.rem(h + step, CHIPS)

    sends = []
    locals_ = []

    def send(src, dst, rsem, device):
        copy = pltpu.make_async_remote_copy(
            src_ref=src, dst_ref=dst, send_sem=ssem.at[len(sends)], recv_sem=rsem,
            device_id=device, device_id_type=MESH,
        )
        sends.append(copy)
        copy.start()
        return copy

    def local(src, dst):
        copy = pltpu.make_async_copy(src, dst, lsem.at[len(locals_)])
        locals_.append(copy)
        copy.start()

    def arrived(dst, rsem):
        pltpu.make_async_copy(dst, dst, rsem).wait()

    barrier = pltpu.get_barrier_semaphore()
    peers = [dev(z, h, other)]
    for step in (1, 2, 3):
        peers += [dev(z, chip(step), 0), dev(z, chip(step), 1)]
    for zz in (z + 1, z - 1):
        peers += [dev(zz, h, 0), dev(zz, h, 1)]
    s_me = lax.axis_index("seq")
    for step in range(1, TENSOR):
        peers.append((s_me, lax.rem(t + step, TENSOR)))
    for peer in peers:
        pl.semaphore_signal(barrier, inc=1, device_id=peer, device_id_type=MESH)

    eye = lax.broadcasted_iota(jnp.int32, (128, 128), 0) == lax.broadcasted_iota(
        jnp.int32, (128, 128), 1
    )
    rows = []
    for ref in (q_ref, k_ref):
        for half in range(2):
            part = ref[half * 128 : (half + 1) * 128, :]
            column = jnp.sum(part * part, axis=1, keepdims=True)
            rows.append(jnp.sum(jnp.where(eye, column, 0.0), axis=0, keepdims=True))
    mine = jnp.concatenate(rows + [jnp.zeros((4, 128), jnp.float32)], axis=0)
    stat[...] = mine
    statr[t] = mine

    pl.semaphore_wait(barrier, len(peers))

    for step in range(1, TENSOR):
        send(stat, statr.at[t], rstat.at[t], (s_me, lax.rem(t + step, TENSOR)))

    def u_slot(position, core):
        return position + 12 - 4 * core

    def spread_u(v, hp, src):
        p = 2 * hp + k
        slot = u_slot(p, other)
        send(src, kvu.at[v, u_slot(p - 8, k)], ru.at[v, u_slot(p - 8, k)], dev(z + 1, h, k))
        send(src, kvu.at[v, u_slot(p + 8, k)], ru.at[v, u_slot(p + 8, k)], dev(z - 1, h, k))
        send(src, kvu.at[v, slot], ru.at[v, slot], dev(z, h, other))

    def spread_4(v, hp, src):
        slot = 8 + 2 * hp + k
        send(src, kv4.at[v, slot - 8], r4.at[v, slot - 8], dev(z + 1, h, k))
        send(src, kv4.at[v, slot + 8], r4.at[v, slot + 8], dev(z - 1, h, k))
        send(src, kv4.at[v, slot], r4.at[v, slot], dev(z, h, other))

    own = 2 * h + k
    relay_to = {0: (1, 0), 1: (3, 1)}

    def first(v, head):
        side, buf = relay_to[v]
        slot = u_slot(own, k)
        send(head(chip(2)), relay.at[buf], rrelay.at[buf], dev(z, chip(side), k))
        for step in (1, 3):
            send(head(chip(step)), kvu.at[v, slot], ru.at[v, slot], dev(z, chip(step), k))
        spread_u(v, h, head(h))
        for step in (1, 3):
            send(head(4), kv4.at[v, 8 + own], r4.at[v, 8 + own], dev(z, chip(step), k))
        spread_4(v, h, head(4))
        local(head(h), kvu.at[v, slot])
        local(head(4), kv4.at[v, 8 + own])

    first(0, lambda i: v_ref.at[:, columns(i)])

    for step in range(1, TENSOR):
        j = lax.rem(t + step, TENSOR)
        arrived(statr.at[j], rstat.at[j])
    total = statr[0]
    for j in range(1, TENSOR):
        total = total + statr[j]
    inverse = 1.0 / jnp.sqrt(total / float(HD * HEADS * TENSOR) + EPS)
    for row, (ref, gain, out) in ((2, (k_ref, kg_ref, kn)), (0, (q_ref, qg_ref, qn))):
        for half in range(2):
            lane_row = inverse[row + half : row + half + 1, :]
            column = jnp.sum(jnp.where(eye, lane_row, 0.0), axis=1, keepdims=True)
            for i in range(HEADS):
                part = ref[half * 128 : (half + 1) * 128, i * HD : (i + 1) * HD]
                out[i, half * 128 : (half + 1) * 128, :] = (
                    part * column * gain[:, i * HD : (i + 1) * HD]
                ).astype(jnp.bfloat16)

    first(1, lambda i: kn.at[i])

    core = lax.div(h, 2)
    place_q = 2 * lax.rem(h, 2) + k
    side_q = chip(1 + 2 * k)
    send(qn.at[chip(2)], relay.at[2], rrelay.at[2], dev(z, side_q, k))
    for step in (1, 3):
        send(qn.at[chip(step)], qu.at[place_q], rq.at[place_q], dev(z, chip(step), core))
    for step in (1, 2, 3):
        send(adj_ref, adju.at[place_q], ra.at[place_q], dev(z, chip(step), core))
    to_self = core == k
    own_q = [
        (qn.at[h], qu.at[place_q], rq.at[place_q]),
        (adj_ref, adju.at[place_q], ra.at[place_q]),
    ]
    cross = len(sends)
    for n, (src, dst, sem) in enumerate(own_q):
        @pl.when(to_self)
        def _():
            pltpu.make_async_copy(src, dst, sem).start()

        @pl.when(jnp.logical_not(to_self))
        def _():
            pltpu.make_async_remote_copy(
                src_ref=src, dst_ref=dst, send_sem=ssem.at[150 + n], recv_sem=sem,
                device_id=dev(z, h, other), device_id_type=MESH,
            ).start()
    local(qn.at[4], q4)

    for v in range(2):
        side, buf = relay_to[v]
        back = chip(4 - side)
        arrived(relay.at[buf], rrelay.at[buf])
        slot = u_slot(2 * back + k, k)
        send(relay.at[buf], kvu.at[v, slot], ru.at[v, slot], dev(z, chip(side), k))
        for step in (1, 3):
            hp = chip(step)
            slot = u_slot(2 * hp + k, k)
            arrived(kvu.at[v, slot], ru.at[v, slot])
            spread_u(v, hp, kvu.at[v, slot])
        for step in (4 - side, side):
            hp = chip(step)
            slot = 8 + 2 * hp + k
            arrived(kv4.at[v, slot], r4.at[v, slot])
            if step == 4 - side:
                send(kv4.at[v, slot], kv4.at[v, slot], r4.at[v, slot], dev(z, chip(side), k))
            spread_4(v, hp, kv4.at[v, slot])
        hp = chip(2)
        slot = u_slot(2 * hp + k, k)
        arrived(kvu.at[v, slot], ru.at[v, slot])
        spread_u(v, hp, kvu.at[v, slot])
        slot = 8 + 2 * hp + k
        arrived(kv4.at[v, slot], r4.at[v, slot])
        spread_4(v, hp, kv4.at[v, slot])

    source = chip(3 - 2 * k)
    arrived(relay.at[2], rrelay.at[2])
    where_q = 2 * lax.rem(source, 2) + k
    send(
        relay.at[2], qu.at[where_q], rq.at[where_q],
        dev(z, lax.rem(source + 2, CHIPS), lax.div(source, 2)),
    )

    for step in (0, 1, 3, 2):
        hp = chip(step)
        up = lax.div(hp, 2)
        sign = 1 - 2 * up
        for v in range(2):
            p = 2 * hp + k
            for q in (p - 8, p + 8):
                slot = u_slot(q, k)
                arrived(kvu.at[v, slot], ru.at[v, slot])
                slot_other = u_slot(q, other)
                send(kvu.at[v, slot], kvu.at[v, slot_other], ru.at[v, slot_other], dev(z, h, other))
            target = u_slot(p + 16 * sign, 1 - up)
            send(
                kvu.at[v, u_slot(p + 8 * sign, k)], kvu.at[v, target], ru.at[v, target],
                dev(z - sign, h, 1 - up),
            )
            for slot in (2 * hp + k, 16 + 2 * hp + k):
                arrived(kv4.at[v, slot], r4.at[v, slot])
                send(kv4.at[v, slot], kv4.at[v, slot], r4.at[v, slot], dev(z, h, other))
            if step == 2:
                send(
                    kv4.at[v, 8 + 8 * sign + 2 * hp + k], kv4.at[v, 24 + k], r4.at[v, 24 + k],
                    dev(z - sign, h, k),
                )

    inner = jnp.logical_or(h == 1, h == 2)
    outer = jnp.logical_or(h == 0, h == 3)
    edge = lax.div(h, 2) * 3
    for v in range(2):
        e0, e1 = 24 + k, 26 + k
        arrived(kv4.at[v, e0], r4.at[v, e0])
        send(kv4.at[v, e0], kv4.at[v, e0], r4.at[v, e0], dev(z, h, other))

        def to_edge():
            return pltpu.make_async_remote_copy(
                src_ref=kv4.at[v, e0], dst_ref=kv4.at[v, e1], send_sem=ssem.at[152 + v],
                recv_sem=r4.at[v, e1], device_id=dev(z, edge, k), device_id_type=MESH,
            )

        def to_partner():
            return pltpu.make_async_remote_copy(
                src_ref=kv4.at[v, e1], dst_ref=kv4.at[v, e1], send_sem=ssem.at[154 + v],
                recv_sem=r4.at[v, e1], device_id=dev(z, h, other), device_id_type=MESH,
            )

        @pl.when(inner)
        def _():
            to_edge().start()

        @pl.when(outer)
        def _():
            arrived(kv4.at[v, e1], r4.at[v, e1])
            to_partner().start()

    for v in range(2):
        for dz in (-1, 0, 1):
            for hp in range(CHIPS):
                slot = u_slot(8 * dz + 2 * hp + other, k)
                arrived(kvu.at[v, slot], ru.at[v, slot])
                slot = 8 + 8 * dz + 2 * hp + other
                arrived(kv4.at[v, slot], r4.at[v, slot])
        for i in range(4):
            arrived(kvu.at[v, 24 * k + i], ru.at[v, 24 * k + i])
        arrived(kv4.at[v, 24 + other], r4.at[v, 24 + other])

        @pl.when(outer)
        def _():
            arrived(kv4.at[v, 26 + other], r4.at[v, 26 + other])

    for i in range(4):
        arrived(qu.at[i], rq.at[i])
        arrived(adju.at[i], ra.at[i])

    for copy in sends:
        copy.wait_send()
    for copy in locals_:
        copy.wait()

    @pl.when(jnp.logical_not(to_self))
    def _():
        for n, (src, dst, sem) in enumerate(own_q):
            pltpu.make_async_copy(src, src, ssem.at[150 + n]).wait()

    for v in range(2):
        @pl.when(inner)
        def _():
            pltpu.make_async_copy(kv4.at[v, 24 + k], kv4.at[v, 24 + k], ssem.at[152 + v]).wait()

        @pl.when(outer)
        def _():
            pltpu.make_async_copy(kv4.at[v, 26 + k], kv4.at[v, 26 + k], ssem.at[154 + v]).wait()


def gather(q_in, k_in, v_in, q_gain, k_gain, adjacent):
    any_space = pl.BlockSpec(memory_space=pl.ANY)
    vmem = pl.BlockSpec(memory_space=pltpu.VMEM)
    bf16 = jnp.bfloat16
    dma = pltpu.SemaphoreType.DMA
    return pl.pallas_call(
        gather_kernel,
        name="gather_window",
        out_shape=(
            jax.ShapeDtypeStruct((2, SLOTS, TOK, HD), bf16),
            jax.ShapeDtypeStruct((2, SLOTS, TOK, HD), bf16),
            jax.ShapeDtypeStruct((4, TOK, HD), bf16),
            jax.ShapeDtypeStruct((TOK, HD), bf16),
            jax.ShapeDtypeStruct((4, 2, 128), jnp.int32),
        ),
        in_specs=[vmem] * 6,
        out_specs=(any_space,) * 5,
        scratch_shapes=[
            pltpu.VMEM((HEADS, TOK, HD), bf16),
            pltpu.VMEM((HEADS, TOK, HD), bf16),
            pltpu.VMEM((8, 128), jnp.float32),
            pltpu.VMEM((TENSOR, 8, 128), jnp.float32),
            pltpu.VMEM((3, TOK, HD), bf16),
            dma((160,)),
            dma((8,)),
            dma((2, SLOTS)),
            dma((2, SLOTS)),
            dma((4,)),
            dma((4,)),
            dma((3,)),
            dma((TENSOR,)),
        ],
        compiler_params=pltpu.CompilerParams(collective_id=0, has_side_effects=True),
    )(q_in, k_in, v_in, q_gain, k_gain, adjacent)


def attend_kernel(frames, adj, adju, qu, q4, kvu, kv4, ou, o4, m_sc, l_sc, acc_sc):
    z, h, k, _ = place()
    lane = lax.broadcasted_iota(jnp.int32, (1, TOK), 1)

    def sweep(q_of, adj_of, s_q, begin, count, key_shard, kv, finish):
        m_sc[...] = jnp.full_like(m_sc, -3e38)
        l_sc[...] = jnp.zeros_like(l_sc)
        acc_sc[...] = jnp.zeros_like(acc_sc)
        fq = [frames[2 * s_q + a] for a in range(2)]

        def tile(n, carry):
            slot = begin + n
            s_k = key_shard(slot)
            valid = jnp.logical_and(s_k >= 0, s_k < 64)
            s_k = jnp.clip(s_k, 0, 63)
            fine = []
            for a in range(2):
                for b in range(2):
                    gap = jnp.abs(fq[a] - frames[2 * s_k + b])
                    near = jnp.logical_and(gap == 1, adj_of(a, 2 * s_k + b) == 1)
                    fine.append(jnp.where(jnp.logical_and(valid, jnp.logical_or(gap == 0, near)), 1, 0))
            @pl.when(fine[0] + fine[1] + fine[2] + fine[3] > 0)
            def _():
                key = kv[1, slot]
                value = kv[0, slot]
                for a in range(2):
                    rows = slice(a * 128, (a + 1) * 128)
                    bias = jnp.where(
                        lane < 128,
                        jnp.where(fine[2 * a] > 0, 0.0, BLOCKED),
                        jnp.where(fine[2 * a + 1] > 0, 0.0, BLOCKED),
                    )
                    s = lax.dot_general(
                        q_of(rows), key, (((1,), (1,)), ((), ())),
                        preferred_element_type=jnp.float32,
                    )
                    s = s * EXP2_SCALE + bias
                    old = m_sc[rows, :]
                    new = jnp.maximum(old, jnp.max(s, axis=1, keepdims=True))
                    fade = jnp.exp2(old - new)
                    p = jnp.exp2(s - new[:, :1])
                    m_sc[rows, :] = new
                    l_sc[rows, :] = l_sc[rows, :] * fade + jnp.sum(p, axis=1, keepdims=True)
                    acc_sc[rows, :] = acc_sc[rows, :] * fade + jnp.dot(
                        p.astype(jnp.bfloat16), value, preferred_element_type=jnp.float32
                    )
            return carry

        lax.fori_loop(0, count, tile, 0)
        finish(acc_sc[...] / l_sc[...])

    def body(i, carry):
        def finish(x):
            ou[i] = x.astype(jnp.bfloat16)

        sweep(
            lambda rows: qu[i, rows, :],
            lambda a, block: adju[i, a, block],
            8 * z + 4 * k + i,
            i,
            25,
            lambda slot: 8 * z + 4 * k + slot - 12,
            kvu,
            finish,
        )
        return carry

    lax.fori_loop(0, 4, body, 0)

    def key_shard(slot):
        side = jnp.where(h < 2, -2, 2)
        e0 = 8 * (z + side) + 2 * lax.rem(h + 2, CHIPS) + slot - 24
        e1 = jnp.where(h == 0, 8 * (z - 2) + 6, jnp.where(h == 3, 8 * (z + 2), -1000)) + slot - 26
        return jnp.where(slot < 24, 8 * z - 8 + slot, jnp.where(slot < 26, e0, e1))

    def finish4(x):
        o4[...] = x

    sweep(
        lambda rows: q4[rows, :],
        lambda a, block: adj[a, block],
        8 * z + 2 * h + k,
        0,
        SLOTS,
        key_shard,
        kv4,
        finish4,
    )


def attend(frames, adjacent, adju, qu, q4, kvu, kv4):
    vmem = pl.BlockSpec(memory_space=pltpu.VMEM)
    smem = pl.BlockSpec(memory_space=pltpu.SMEM)
    return pl.pallas_call(
        attend_kernel,
        name="attend",
        out_shape=(
            jax.ShapeDtypeStruct((4, TOK, HD), jnp.bfloat16),
            jax.ShapeDtypeStruct((TOK, HD), jnp.float32),
        ),
        in_specs=[smem] * 3 + [vmem] * 4,
        out_specs=(vmem, vmem),
        scratch_shapes=[pltpu.VMEM((TOK, HD), jnp.float32)] * 3,
    )(frames, adjacent, adju, qu, q4, kvu, kv4)


def return_kernel(ou, o4, out, rbuf, ssem, rsem):
    z, h, k, t = place()
    other = 1 - k

    def dev(hh, kk):
        return (z * 8 + hh * 2 + kk, t)

    def chip(step):
        return lax.rem(h + step, CHIPS)

    barrier = pltpu.get_barrier_semaphore()
    peers = [dev(h, other)]
    for step in (1, 2, 3):
        peers += [dev(chip(step), 0), dev(chip(step), 1)]
    for peer in peers:
        pl.semaphore_signal(barrier, inc=1, device_id=peer, device_id_type=MESH)
    out[:, 4 * HD :] = o4[...]
    pl.semaphore_wait(barrier, len(peers))

    for i in range(4):
        hh, kk = 2 * k + i // 2, i % 2
        mine = jnp.logical_and(hh == h, kk == k)

        @pl.when(mine)
        def _():
            pltpu.make_async_copy(ou.at[i], rbuf.at[h], rsem.at[h]).start()

        @pl.when(jnp.logical_not(mine))
        def _():
            pltpu.make_async_remote_copy(
                src_ref=ou.at[i], dst_ref=rbuf.at[h], send_sem=ssem.at[i], recv_sem=rsem.at[h],
                device_id=dev(hh, kk), device_id_type=MESH,
            ).start()

    for i in range(4):
        pltpu.make_async_copy(rbuf.at[i], rbuf.at[i], rsem.at[i]).wait()
        out[:, i * HD : (i + 1) * HD] = rbuf[i].astype(jnp.float32)

    for i in range(4):
        hh, kk = 2 * k + i // 2, i % 2
        mine = jnp.logical_and(hh == h, kk == k)

        @pl.when(jnp.logical_not(mine))
        def _():
            pltpu.make_async_copy(ou.at[i], ou.at[i], ssem.at[i]).wait()


def give_back(ou, o4):
    vmem = pl.BlockSpec(memory_space=pltpu.VMEM)
    return pl.pallas_call(
        return_kernel,
        name="give_back",
        out_shape=jax.ShapeDtypeStruct((TOK, HEADS * HD), jnp.float32),
        in_specs=[vmem] * 2,
        out_specs=vmem,
        scratch_shapes=[
            pltpu.VMEM((4, TOK, HD), jnp.bfloat16),
            pltpu.SemaphoreType.DMA((4,)),
            pltpu.SemaphoreType.DMA((4,)),
        ],
        compiler_params=pltpu.CompilerParams(collective_id=1, has_side_effects=True),
    )(ou, o4)


def shards(q_in, k_in, v_in, q_gain, k_gain, frames, adjacent):
    kvu, kv4, qu, q4, adju = gather(
        q_in, k_in, v_in, q_gain[None, :], k_gain[None, :], adjacent
    )
    ou, o4 = attend(frames, adjacent, adju, qu, q4, kvu, kv4)
    return give_back(ou, o4)


def solution(mesh):
    return jax.shard_map(
        shards,
        mesh=mesh,
        in_specs=(
            P("seq", "tensor"),
            P("seq", "tensor"),
            P("seq", "tensor"),
            P("tensor"),
            P("tensor"),
            P(),
            P("seq", None),
        ),
        out_specs=P("seq", "tensor"),
        check_vma=False,
    )
```

```python
import math

import jax
import jax.numpy as jnp
from jax import lax
from jax.experimental import pallas as pl
from jax.experimental.pallas import tpu as pltpu
from jax.sharding import PartitionSpec as P

HD = 128
TOK = 256
HEADS = 5
CHIPS = 4
PLANES = 8
TENSOR = 8
SLOTS = 28
MESH = pl.DeviceIdType.MESH
EPS = 1e-06
BLOCKED = -1e30
EXP2_SCALE = math.log2(math.e) / math.sqrt(HD)


def place():
    s = lax.axis_index("seq")
    return lax.div(s, 8), lax.rem(lax.div(s, 2), 4), lax.rem(s, 2), lax.axis_index("tensor")


def gather_kernel(
    q_ref, k_ref, v_ref, qg_ref, kg_ref, adj_ref,
    vu, ku, v4, k4, qu, q4, adju,
    qn, kn, vt, stat, statr, relay_v, relay_k, relay_q,
    ssem, lsem, ru, r4, rq, ra, rrelay, rstat,
):
    z, h, k, t = place()
    other = 1 - k
    kvu, kv4 = (vu, ku), (v4, k4)
    relay = (relay_v, relay_k, relay_q)

    def dev(zz, hh, kk):
        return (lax.rem(zz + PLANES, PLANES) * 8 + hh * 2 + kk, t)

    def chip(step):
        return lax.rem(h + step, CHIPS)

    sends = []
    locals_ = []

    def send(src, dst, rsem, device):
        copy = pltpu.make_async_remote_copy(
            src_ref=src, dst_ref=dst, send_sem=ssem.at[len(sends)], recv_sem=rsem,
            device_id=device, device_id_type=MESH,
        )
        sends.append(copy)
        copy.start()
        return copy

    def local(src, dst):
        copy = pltpu.make_async_copy(src, dst, lsem.at[len(locals_)])
        locals_.append(copy)
        copy.start()

    def arrived(dst, rsem):
        pltpu.make_async_copy(dst, dst, rsem).wait()

    barrier = pltpu.get_barrier_semaphore()
    peers = [dev(z, h, other)]
    for step in (1, 2, 3):
        peers += [dev(z, chip(step), 0), dev(z, chip(step), 1)]
    for zz in (z + 1, z - 1):
        peers += [dev(zz, h, 0), dev(zz, h, 1)]
    s_me = lax.axis_index("seq")
    for step in range(1, TENSOR):
        peers.append((s_me, lax.rem(t + step, TENSOR)))
    for peer in peers:
        pl.semaphore_signal(barrier, inc=1, device_id=peer, device_id_type=MESH)

    eye = lax.broadcasted_iota(jnp.int32, (128, 128), 0) == lax.broadcasted_iota(
        jnp.int32, (128, 128), 1
    )
    rows = []
    for ref in (q_ref, k_ref):
        for half in range(2):
            part = ref[half * 128 : (half + 1) * 128, :]
            column = jnp.sum(part * part, axis=1, keepdims=True)
            rows.append(jnp.sum(jnp.where(eye, column, 0.0), axis=0, keepdims=True))
    mine = jnp.concatenate(rows + [jnp.zeros((4, 128), jnp.float32)], axis=0)
    stat[...] = mine
    statr[t] = mine
    for i in range(HEADS):
        vt[i] = v_ref[:, i * HD : (i + 1) * HD].T

    pl.semaphore_wait(barrier, len(peers))

    for step in range(1, TENSOR):
        send(stat, statr.at[t], rstat.at[t], (s_me, lax.rem(t + step, TENSOR)))

    def u_slot(position, core):
        return position + 12 - 4 * core

    def spread_u(v, hp, src):
        p = 2 * hp + k
        slot = u_slot(p, other)
        send(src, kvu[v].at[u_slot(p - 8, k)], ru.at[v, u_slot(p - 8, k)], dev(z + 1, h, k))
        send(src, kvu[v].at[u_slot(p + 8, k)], ru.at[v, u_slot(p + 8, k)], dev(z - 1, h, k))
        send(src, kvu[v].at[slot], ru.at[v, slot], dev(z, h, other))

    def spread_4(v, hp, src):
        slot = 8 + 2 * hp + k
        send(src, kv4[v].at[slot - 8], r4.at[v, slot - 8], dev(z + 1, h, k))
        send(src, kv4[v].at[slot + 8], r4.at[v, slot + 8], dev(z - 1, h, k))
        send(src, kv4[v].at[slot], r4.at[v, slot], dev(z, h, other))

    own = 2 * h + k
    relay_to = {0: (1, 0), 1: (3, 1)}

    def first(v, head):
        side, buf = relay_to[v]
        slot = u_slot(own, k)
        send(head(chip(2)), relay[buf], rrelay.at[buf], dev(z, chip(side), k))
        for step in (1, 3):
            send(head(chip(step)), kvu[v].at[slot], ru.at[v, slot], dev(z, chip(step), k))
        spread_u(v, h, head(h))
        for step in (1, 3):
            send(head(4), kv4[v].at[8 + own], r4.at[v, 8 + own], dev(z, chip(step), k))
        spread_4(v, h, head(4))
        local(head(h), kvu[v].at[slot])
        local(head(4), kv4[v].at[8 + own])

    first(0, lambda i: vt.at[i])

    for step in range(1, TENSOR):
        j = lax.rem(t + step, TENSOR)
        arrived(statr.at[j], rstat.at[j])
    total = statr[0]
    for j in range(1, TENSOR):
        total = total + statr[j]
    inverse = 1.0 / jnp.sqrt(total / float(HD * HEADS * TENSOR) + EPS)
    for row, ref, gain in ((2, k_ref, kg_ref), (0, q_ref, qg_ref)):
        for half in range(2):
            lane_row = inverse[row + half : row + half + 1, :]
            column = jnp.sum(jnp.where(eye, lane_row, 0.0), axis=1, keepdims=True)
            span = slice(half * 128, (half + 1) * 128)
            for i in range(HEADS):
                feature = slice(i * HD, (i + 1) * HD)
                part = ref[span, feature] * column * gain[feature][None, :]
                if row == 2:
                    kn[i, span, :] = part.astype(jnp.bfloat16)
                else:
                    qn[i, :, span] = part.T.astype(jnp.bfloat16)

    first(1, lambda i: kn.at[i])

    core = lax.div(h, 2)
    place_q = 2 * lax.rem(h, 2) + k
    side_q = chip(1 + 2 * k)
    send(qn.at[chip(2)], relay[2], rrelay.at[2], dev(z, side_q, k))
    for step in (1, 3):
        send(qn.at[chip(step)], qu.at[place_q], rq.at[place_q], dev(z, chip(step), core))
    for step in (1, 2, 3):
        send(adj_ref, adju.at[place_q], ra.at[place_q], dev(z, chip(step), core))
    to_self = core == k
    own_q = [
        (qn.at[h], qu.at[place_q], rq.at[place_q]),
        (adj_ref, adju.at[place_q], ra.at[place_q]),
    ]
    cross = len(sends)
    for n, (src, dst, sem) in enumerate(own_q):
        @pl.when(to_self)
        def _():
            pltpu.make_async_copy(src, dst, sem).start()

        @pl.when(jnp.logical_not(to_self))
        def _():
            pltpu.make_async_remote_copy(
                src_ref=src, dst_ref=dst, send_sem=ssem.at[150 + n], recv_sem=sem,
                device_id=dev(z, h, other), device_id_type=MESH,
            ).start()
    local(qn.at[4], q4)

    for v in range(2):
        side, buf = relay_to[v]
        back = chip(4 - side)
        arrived(relay[buf], rrelay.at[buf])
        slot = u_slot(2 * back + k, k)
        send(relay[buf], kvu[v].at[slot], ru.at[v, slot], dev(z, chip(side), k))
        for step in (1, 3):
            hp = chip(step)
            slot = u_slot(2 * hp + k, k)
            arrived(kvu[v].at[slot], ru.at[v, slot])
            spread_u(v, hp, kvu[v].at[slot])
        for step in (4 - side, side):
            hp = chip(step)
            slot = 8 + 2 * hp + k
            arrived(kv4[v].at[slot], r4.at[v, slot])
            if step == 4 - side:
                send(kv4[v].at[slot], kv4[v].at[slot], r4.at[v, slot], dev(z, chip(side), k))
            spread_4(v, hp, kv4[v].at[slot])
        hp = chip(2)
        slot = u_slot(2 * hp + k, k)
        arrived(kvu[v].at[slot], ru.at[v, slot])
        spread_u(v, hp, kvu[v].at[slot])
        slot = 8 + 2 * hp + k
        arrived(kv4[v].at[slot], r4.at[v, slot])
        spread_4(v, hp, kv4[v].at[slot])

    source = chip(3 - 2 * k)
    arrived(relay[2], rrelay.at[2])
    where_q = 2 * lax.rem(source, 2) + k
    send(
        relay[2], qu.at[where_q], rq.at[where_q],
        dev(z, lax.rem(source + 2, CHIPS), lax.div(source, 2)),
    )

    for step in (0, 1, 3, 2):
        hp = chip(step)
        up = lax.div(hp, 2)
        sign = 1 - 2 * up
        for v in range(2):
            p = 2 * hp + k
            for q in (p - 8, p + 8):
                slot = u_slot(q, k)
                arrived(kvu[v].at[slot], ru.at[v, slot])
                slot_other = u_slot(q, other)
                send(kvu[v].at[slot], kvu[v].at[slot_other], ru.at[v, slot_other], dev(z, h, other))
            target = u_slot(p + 16 * sign, 1 - up)
            send(
                kvu[v].at[u_slot(p + 8 * sign, k)], kvu[v].at[target], ru.at[v, target],
                dev(z - sign, h, 1 - up),
            )
            for slot in (2 * hp + k, 16 + 2 * hp + k):
                arrived(kv4[v].at[slot], r4.at[v, slot])
                send(kv4[v].at[slot], kv4[v].at[slot], r4.at[v, slot], dev(z, h, other))
            if step == 2:
                send(
                    kv4[v].at[8 + 8 * sign + 2 * hp + k], kv4[v].at[24 + k], r4.at[v, 24 + k],
                    dev(z - sign, h, k),
                )

    inner = jnp.logical_or(h == 1, h == 2)
    outer = jnp.logical_or(h == 0, h == 3)
    edge = lax.div(h, 2) * 3
    for v in range(2):
        e0, e1 = 24 + k, 26 + k
        arrived(kv4[v].at[e0], r4.at[v, e0])
        send(kv4[v].at[e0], kv4[v].at[e0], r4.at[v, e0], dev(z, h, other))

        def to_edge():
            return pltpu.make_async_remote_copy(
                src_ref=kv4[v].at[e0], dst_ref=kv4[v].at[e1], send_sem=ssem.at[152 + v],
                recv_sem=r4.at[v, e1], device_id=dev(z, edge, k), device_id_type=MESH,
            )

        def to_partner():
            return pltpu.make_async_remote_copy(
                src_ref=kv4[v].at[e1], dst_ref=kv4[v].at[e1], send_sem=ssem.at[154 + v],
                recv_sem=r4.at[v, e1], device_id=dev(z, h, other), device_id_type=MESH,
            )

        @pl.when(inner)
        def _():
            to_edge().start()

        @pl.when(outer)
        def _():
            arrived(kv4[v].at[e1], r4.at[v, e1])
            to_partner().start()

    for v in range(2):
        for dz in (-1, 0, 1):
            for hp in range(CHIPS):
                slot = u_slot(8 * dz + 2 * hp + other, k)
                arrived(kvu[v].at[slot], ru.at[v, slot])
                slot = 8 + 8 * dz + 2 * hp + other
                arrived(kv4[v].at[slot], r4.at[v, slot])
        for i in range(4):
            arrived(kvu[v].at[24 * k + i], ru.at[v, 24 * k + i])
        arrived(kv4[v].at[24 + other], r4.at[v, 24 + other])

        @pl.when(outer)
        def _():
            arrived(kv4[v].at[26 + other], r4.at[v, 26 + other])

    for i in range(4):
        arrived(qu.at[i], rq.at[i])
        arrived(adju.at[i], ra.at[i])

    for copy in sends:
        copy.wait_send()
    for copy in locals_:
        copy.wait()

    @pl.when(jnp.logical_not(to_self))
    def _():
        for n, (src, dst, sem) in enumerate(own_q):
            pltpu.make_async_copy(src, src, ssem.at[150 + n]).wait()

    for v in range(2):
        @pl.when(inner)
        def _():
            pltpu.make_async_copy(kv4[v].at[24 + k], kv4[v].at[24 + k], ssem.at[152 + v]).wait()

        @pl.when(outer)
        def _():
            pltpu.make_async_copy(kv4[v].at[26 + k], kv4[v].at[26 + k], ssem.at[154 + v]).wait()


def gather(q_in, k_in, v_in, q_gain, k_gain, adjacent):
    any_space = pl.BlockSpec(memory_space=pl.ANY)
    vmem = pl.BlockSpec(memory_space=pltpu.VMEM)
    bf16 = jnp.bfloat16
    dma = pltpu.SemaphoreType.DMA
    return pl.pallas_call(
        gather_kernel,
        name="gather_window",
        out_shape=(
            jax.ShapeDtypeStruct((SLOTS, HD, TOK), bf16),
            jax.ShapeDtypeStruct((SLOTS, TOK, HD), bf16),
            jax.ShapeDtypeStruct((SLOTS, HD, TOK), bf16),
            jax.ShapeDtypeStruct((SLOTS, TOK, HD), bf16),
            jax.ShapeDtypeStruct((4, HD, TOK), bf16),
            jax.ShapeDtypeStruct((HD, TOK), bf16),
            jax.ShapeDtypeStruct((4, 2, 128), jnp.int32),
        ),
        in_specs=[vmem] * 6,
        out_specs=(any_space,) * 7,
        scratch_shapes=[
            pltpu.VMEM((HEADS, HD, TOK), bf16),
            pltpu.VMEM((HEADS, TOK, HD), bf16),
            pltpu.VMEM((HEADS, HD, TOK), bf16),
            pltpu.VMEM((8, 128), jnp.float32),
            pltpu.VMEM((TENSOR, 8, 128), jnp.float32),
            pltpu.VMEM((HD, TOK), bf16),
            pltpu.VMEM((TOK, HD), bf16),
            pltpu.VMEM((HD, TOK), bf16),
            dma((160,)),
            dma((8,)),
            dma((2, SLOTS)),
            dma((2, SLOTS)),
            dma((4,)),
            dma((4,)),
            dma((3,)),
            dma((TENSOR,)),
        ],
        compiler_params=pltpu.CompilerParams(collective_id=0, has_side_effects=True),
    )(q_in, k_in, v_in, q_gain, k_gain, adjacent)


def fold(tiles, m_sc, l_sc, acc_sc):
    halves = (slice(0, 128), slice(128, 256))
    for state, queries, keys, values, bias in tiles:
        scores = jnp.dot(keys, queries, preferred_element_type=jnp.float32)
        weights, news, sums = [], [], []
        for a in range(2):
            old = m_sc[state, :, halves[a]]
            new = old
            for b in range(2):
                top = jnp.max(scores[halves[b], halves[a]], axis=0, keepdims=True)
                new = jnp.maximum(new, top * EXP2_SCALE + bias[a][b])
            parts = [
                jnp.exp2(scores[halves[b], halves[a]] * EXP2_SCALE - (new - bias[a][b]))
                for b in range(2)
            ]
            column = jnp.concatenate(parts, axis=0)
            sums.append(jnp.sum(column, axis=0, keepdims=True))
            weights.append(column.astype(jnp.bfloat16))
            news.append(new)
        new = jnp.concatenate(news, axis=1)
        fade = jnp.exp2(m_sc[state] - new)
        m_sc[state] = new
        l_sc[state] = l_sc[state] * fade + jnp.concatenate(sums, axis=1)
        mixed = jnp.dot(
            values, jnp.concatenate(weights, axis=1), preferred_element_type=jnp.float32
        )
        acc_sc[state] = acc_sc[state] * fade + mixed


def attend_kernel(frames, adj, adju, qu, q4, vu, ku, v4, k4, ou, o4, bias_v, bias_s, sem, m_sc, l_sc, acc_sc):
    z, h, k, _ = place()

    frame_row = frames[...][None, :]
    lane = lax.broadcasted_iota(jnp.int32, (1, 128), 1)
    rows = []
    for i in range(5):
        shard = 8 * z + 4 * k + i if i < 4 else 8 * z + 2 * h + k
        for a in range(2):
            mine = jnp.max(jnp.where(lane == 2 * shard + a, frame_row, -1), axis=1, keepdims=True)
            gap = jnp.abs(frame_row - mine)
            linked = (adju[i, a : a + 1, :] if i < 4 else adj[a : a + 1, :]) == 1
            fine = (gap == 0) | ((gap == 1) & linked)
            rows.append(jnp.where(fine, 0.0, BLOCKED))
    bias_v[...] = jnp.concatenate(rows + [jnp.zeros((6, 128), jnp.float32)], axis=0)
    copy = pltpu.make_async_copy(bias_v, bias_s, sem)
    copy.start()
    m_sc[...] = jnp.full_like(m_sc, -1e29)
    l_sc[...] = jnp.zeros_like(l_sc)
    acc_sc[...] = jnp.zeros_like(acc_sc)
    copy.wait()

    def bias_of(i, shard):
        valid = jnp.logical_and(shard >= 0, shard < 64)
        at = jnp.clip(shard, 0, 63)
        return [
            [jnp.where(valid, bias_s[2 * i + a, 2 * at + b], BLOCKED) for b in range(2)]
            for a in range(2)
        ]

    def needed(biases):
        best = jnp.float32(BLOCKED)
        for bias in biases:
            for row in bias:
                for value in row:
                    best = jnp.maximum(best, value)
        return best == 0.0

    def u_group(slot, carry):
        shard = 8 * z + 4 * k + slot - 12
        biases = [bias_of(i, shard) for i in range(4)]

        @pl.when(needed(biases))
        def _():
            fold(
                [(i, qu[i], ku[slot], vu[slot], biases[i]) for i in range(4)],
                m_sc, l_sc, acc_sc,
            )

        return carry

    def key_shard(slot):
        side = jnp.where(h < 2, -2, 2)
        e0 = 8 * (z + side) + 2 * lax.rem(h + 2, CHIPS) + slot - 24
        e1 = jnp.where(h == 0, 8 * (z - 2) + 6, jnp.where(h == 3, 8 * (z + 2), -1000)) + slot - 26
        return jnp.where(slot < 24, 8 * z - 8 + slot, jnp.where(slot < 26, e0, e1))

    def h4_group(slot, carry):
        bias = bias_of(4, key_shard(slot))

        @pl.when(needed([bias]))
        def _():
            fold([(4, q4[...], k4[slot], v4[slot], bias)], m_sc, l_sc, acc_sc)

        return carry

    lax.fori_loop(0, SLOTS, u_group, 0)
    lax.fori_loop(0, SLOTS, h4_group, 0)
    for i in range(4):
        ou[i] = (acc_sc[i] / l_sc[i]).T.astype(jnp.bfloat16)
    o4[...] = (acc_sc[4] / l_sc[4]).T


def attend(frames, adjacent, adju, qu, q4, vu, ku, v4, k4):
    vmem = pl.BlockSpec(memory_space=pltpu.VMEM)
    f32 = jnp.float32
    return pl.pallas_call(
        attend_kernel,
        name="attend",
        out_shape=(
            jax.ShapeDtypeStruct((4, TOK, HD), jnp.bfloat16),
            jax.ShapeDtypeStruct((TOK, HD), f32),
        ),
        in_specs=[vmem] * 9,
        out_specs=(vmem, vmem),
        scratch_shapes=[
            pltpu.VMEM((16, 128), f32),
            pltpu.SMEM((16, 128), f32),
            pltpu.SemaphoreType.DMA,
            pltpu.VMEM((5, 1, TOK), f32),
            pltpu.VMEM((5, 1, TOK), f32),
            pltpu.VMEM((5, HD, TOK), f32),
        ],
    )(frames, adjacent, adju, qu, q4, vu, ku, v4, k4)


def return_kernel(ou, o4, out, rbuf, ssem, rsem):
    z, h, k, t = place()
    other = 1 - k

    def dev(hh, kk):
        return (z * 8 + hh * 2 + kk, t)

    def chip(step):
        return lax.rem(h + step, CHIPS)

    barrier = pltpu.get_barrier_semaphore()
    peers = [dev(h, other)]
    for step in (1, 2, 3):
        peers += [dev(chip(step), 0), dev(chip(step), 1)]
    for peer in peers:
        pl.semaphore_signal(barrier, inc=1, device_id=peer, device_id_type=MESH)
    out[:, 4 * HD :] = o4[...]
    pl.semaphore_wait(barrier, len(peers))

    for i in range(4):
        hh, kk = 2 * k + i // 2, i % 2
        mine = jnp.logical_and(hh == h, kk == k)

        @pl.when(mine)
        def _():
            pltpu.make_async_copy(ou.at[i], rbuf.at[h], rsem.at[h]).start()

        @pl.when(jnp.logical_not(mine))
        def _():
            pltpu.make_async_remote_copy(
                src_ref=ou.at[i], dst_ref=rbuf.at[h], send_sem=ssem.at[i], recv_sem=rsem.at[h],
                device_id=dev(hh, kk), device_id_type=MESH,
            ).start()

    for i in range(4):
        pltpu.make_async_copy(rbuf.at[i], rbuf.at[i], rsem.at[i]).wait()
        out[:, i * HD : (i + 1) * HD] = rbuf[i].astype(jnp.float32)

    for i in range(4):
        hh, kk = 2 * k + i // 2, i % 2
        mine = jnp.logical_and(hh == h, kk == k)

        @pl.when(jnp.logical_not(mine))
        def _():
            pltpu.make_async_copy(ou.at[i], ou.at[i], ssem.at[i]).wait()


def give_back(ou, o4):
    vmem = pl.BlockSpec(memory_space=pltpu.VMEM)
    return pl.pallas_call(
        return_kernel,
        name="give_back",
        out_shape=jax.ShapeDtypeStruct((TOK, HEADS * HD), jnp.float32),
        in_specs=[vmem] * 2,
        out_specs=vmem,
        scratch_shapes=[
            pltpu.VMEM((4, TOK, HD), jnp.bfloat16),
            pltpu.SemaphoreType.DMA((4,)),
            pltpu.SemaphoreType.DMA((4,)),
        ],
        compiler_params=pltpu.CompilerParams(collective_id=1, has_side_effects=True),
    )(ou, o4)


def shards(q_in, k_in, v_in, q_gain, k_gain, frames, adjacent):
    vu, ku, v4, k4, qu, q4, adju = gather(q_in, k_in, v_in, q_gain, k_gain, adjacent)
    ou, o4 = attend(frames, adjacent, adju, qu, q4, vu, ku, v4, k4)
    return give_back(ou, o4)


def solution(mesh):
    return jax.shard_map(
        shards,
        mesh=mesh,
        in_specs=(
            P("seq", "tensor"),
            P("seq", "tensor"),
            P("seq", "tensor"),
            P("tensor"),
            P("tensor"),
            P(),
            P("seq", None),
        ),
        out_specs=P("seq", "tensor"),
        check_vma=False,
    )
```

```python
import math

import jax
import jax.numpy as jnp
from jax import lax
from jax.experimental import pallas as pl
from jax.experimental.pallas import tpu as pltpu
from jax.sharding import PartitionSpec as P

HD = 128
TOK = 256
HEADS = 5
CHIPS = 4
PLANES = 8
TENSOR = 8
SLOTS = 28
MESH = pl.DeviceIdType.MESH
EPS = 1e-06
BLOCKED = -1e30
EXP2_SCALE = math.log2(math.e) / math.sqrt(HD)


def place():
    s = lax.axis_index("seq")
    return lax.div(s, 8), lax.rem(lax.div(s, 2), 4), lax.rem(s, 2), lax.axis_index("tensor")


def fold(tiles, m_sc, l_sc, acc_sc):
    halves = (slice(0, 128), slice(128, 256))
    count = len(tiles)
    scores, weights, fades, sums = {}, {}, {}, {}

    def score(n):
        state, queries, keys, values, bias = tiles[n]
        scores[n] = jnp.dot(keys, queries, preferred_element_type=jnp.float32)

    def weigh(n):
        state, queries, keys, values, bias = tiles[n]
        s = scores.pop(n)
        blocks = s.shape[0] // 128
        columns, news, totals = [], [], []
        for a in range(2):
            new = m_sc[state, :, halves[a]]
            for b in range(blocks):
                top = jnp.max(s[b * 128 : (b + 1) * 128, halves[a]], axis=0, keepdims=True)
                new = jnp.maximum(new, top * EXP2_SCALE + bias[a][b])
            parts = [
                jnp.exp2(s[b * 128 : (b + 1) * 128, halves[a]] * EXP2_SCALE - (new - bias[a][b]))
                for b in range(blocks)
            ]
            column = jnp.concatenate(parts, axis=0)
            totals.append(jnp.sum(column, axis=0, keepdims=True))
            columns.append(column.astype(jnp.bfloat16))
            news.append(new)
        new = jnp.concatenate(news, axis=1)
        fades[n] = jnp.exp2(m_sc[state] - new)
        m_sc[state] = new
        l_sc[state] = l_sc[state] * fades[n] + jnp.concatenate(totals, axis=1)
        weights[n] = jnp.concatenate(columns, axis=1)

    def mix(n):
        state, queries, keys, values, bias = tiles[n]
        mixed = jnp.dot(values, weights.pop(n), preferred_element_type=jnp.float32)
        acc_sc[state] = acc_sc[state] * fades.pop(n) + mixed

    score(0)
    for n in range(count):
        if n + 1 < count:
            score(n + 1)
        if n > 0:
            mix(n - 1)
        weigh(n)
    mix(count - 1)


def kernel(
    q_ref, k_ref, v_ref, qg_ref, kg_ref, adj_ref, frames_ref,
    out_ref,
    vu, ku, v4, k4, qu, adju, qn, kn, vt, stat, statr, relay_v, relay_k, relay_q,
    bias_v, bias_s, m_sc, l_sc, acc_sc, obuf, rbuf,
    ssem, bsem, ru, r4, rq, ra, rrelay, rstat, ro,
):
    z, h, k, t = place()
    other = 1 - k
    kvu, kv4 = (vu, ku), (v4, k4)
    relay = (relay_v, relay_k, relay_q)
    s_me = lax.axis_index("seq")
    inner = jnp.logical_or(h == 1, h == 2)
    outer = jnp.logical_or(h == 0, h == 3)

    def dev(zz, hh, kk):
        return (lax.rem(zz + PLANES, PLANES) * 8 + hh * 2 + kk, t)

    def chip(step):
        return lax.rem(h + step, CHIPS)

    sends = []

    def send(src, dst, rsem, device):
        copy = pltpu.make_async_remote_copy(
            src_ref=src, dst_ref=dst, send_sem=ssem.at[len(sends)], recv_sem=rsem,
            device_id=device, device_id_type=MESH,
        )
        sends.append((copy, None))
        copy.start()

    def send_if(condition, src, dst, rsem, device):
        copy = pltpu.make_async_remote_copy(
            src_ref=src, dst_ref=dst, send_sem=ssem.at[len(sends)], recv_sem=rsem,
            device_id=device, device_id_type=MESH,
        )
        sends.append((copy, condition))

        @pl.when(condition)
        def _():
            copy.start()

    def arrived(dst, rsem):
        pltpu.make_async_copy(dst, dst, rsem).wait()

    for ref in (v4, k4):
        for slot in (26, 27):
            ref[slot] = jnp.zeros(ref.shape[1:], ref.dtype)

    barrier = pltpu.get_barrier_semaphore()
    peers = [dev(z, h, other)]
    for step in (1, 2, 3):
        peers += [dev(z, chip(step), 0), dev(z, chip(step), 1)]
    for zz in (z + 1, z - 1):
        peers += [dev(zz, h, 0), dev(zz, h, 1)]
    for step in range(1, TENSOR):
        peers.append((s_me, lax.rem(t + step, TENSOR)))
    for peer in peers:
        pl.semaphore_signal(barrier, inc=1, device_id=peer, device_id_type=MESH)

    eye = lax.broadcasted_iota(jnp.int32, (128, 128), 0) == lax.broadcasted_iota(
        jnp.int32, (128, 128), 1
    )
    rows = []
    for ref in (q_ref, k_ref):
        for half in range(2):
            part = ref[half * 128 : (half + 1) * 128, :]
            column = jnp.sum(part * part, axis=1, keepdims=True)
            rows.append(jnp.sum(jnp.where(eye, column, 0.0), axis=0, keepdims=True))
    mine = jnp.concatenate(rows + [jnp.zeros((4, 128), jnp.float32)], axis=0)
    stat[...] = mine
    statr[t] = mine

    def u_slot(position, core):
        return position + 12 - 4 * core

    own = 2 * h + k
    for i in range(HEADS):
        vt[i] = v_ref[:, i * HD : (i + 1) * HD].T
    vu[u_slot(own, k)] = vt[h]
    v4[8 + own] = vt[4]
    m_sc[...] = jnp.full_like(m_sc, -1e29)
    l_sc[...] = jnp.zeros_like(l_sc)
    acc_sc[...] = jnp.zeros_like(acc_sc)

    pl.semaphore_wait(barrier, len(peers))

    for step in range(1, TENSOR):
        send(stat, statr.at[t], rstat.at[t], (s_me, lax.rem(t + step, TENSOR)))

    def spread_u(v, hp, src):
        p = 2 * hp + k
        slot = u_slot(p, other)
        up, down = u_slot(p - 8, k), u_slot(p + 8, k)
        send(src, kvu[v].at[up], ru.at[v, up], dev(z + 1, h, k))
        send(src, kvu[v].at[down], ru.at[v, down], dev(z - 1, h, k))
        send(src, kvu[v].at[slot], ru.at[v, slot], dev(z, h, other))

    def spread_4(v, hp, src):
        slot = 8 + 2 * hp + k
        send(src, kv4[v].at[slot - 8], r4.at[v, slot - 8], dev(z + 1, h, k))
        send(src, kv4[v].at[slot + 8], r4.at[v, slot + 8], dev(z - 1, h, k))
        send(src, kv4[v].at[slot], r4.at[v, slot], dev(z, h, other))

    relay_to = {0: (1, 0), 1: (3, 1)}

    def first_y(v, ref):
        side, buf = relay_to[v]
        slot = u_slot(own, k)
        send(ref.at[chip(2)], relay[buf], rrelay.at[buf], dev(z, chip(side), k))
        for step in (1, 3):
            send(ref.at[chip(step)], kvu[v].at[slot], ru.at[v, slot], dev(z, chip(step), k))
        for step in (1, 3):
            send(ref.at[4], kv4[v].at[8 + own], r4.at[v, 8 + own], dev(z, chip(step), k))

    def first_z(v, ref):
        spread_u(v, h, ref.at[h])
        spread_4(v, h, ref.at[4])

    first_y(0, vt)
    first_z(0, vt)

    core = lax.div(h, 2)
    place_q = 2 * lax.rem(h, 2) + k
    to_self = core == k
    to_other = jnp.logical_not(to_self)
    for step in (1, 2, 3):
        send(adj_ref, adju.at[place_q], ra.at[place_q], dev(z, chip(step), core))
    send_if(to_other, adj_ref, adju.at[place_q], ra.at[place_q], dev(z, h, other))

    for step in range(1, TENSOR):
        j = lax.rem(t + step, TENSOR)
        arrived(statr.at[j], rstat.at[j])
    total = statr[0]
    for j in range(1, TENSOR):
        total = total + statr[j]
    inverse = 1.0 / jnp.sqrt(total / float(HD * HEADS * TENSOR) + EPS)

    def normalize(row, ref, gain, put):
        for half in range(2):
            lane_row = inverse[row + half : row + half + 1, :]
            column = jnp.sum(jnp.where(eye, lane_row, 0.0), axis=1, keepdims=True)
            span = slice(half * 128, (half + 1) * 128)
            for i in range(HEADS):
                feature = slice(i * HD, (i + 1) * HD)
                put(i, span, ref[span, feature] * column * gain[feature][None, :])

    def put_k(i, span, x):
        kn[i, span, :] = x.astype(jnp.bfloat16)

    def put_q(i, span, x):
        qn[i, :, span] = x.T.astype(jnp.bfloat16)

    normalize(2, k_ref, kg_ref, put_k)
    normalize(0, q_ref, qg_ref, put_q)
    ku[u_slot(own, k)] = kn[h]
    k4[8 + own] = kn[4]
    first_z(1, kn)

    send(qn.at[chip(2)], relay[2], rrelay.at[2], dev(z, chip(1 + 2 * k), k))
    for step in (1, 3):
        send(qn.at[chip(step)], qu.at[place_q], rq.at[place_q], dev(z, chip(step), core))
    send_if(to_other, qn.at[h], qu.at[place_q], rq.at[place_q], dev(z, h, other))

    @pl.when(to_self)
    def _():
        qu[place_q] = qn[h]
        adju[place_q] = adj_ref[...]

    first_y(1, kn)

    def pass_relay(v):
        side, buf = relay_to[v]
        arrived(relay[buf], rrelay.at[buf])
        slot = u_slot(2 * chip(4 - side) + k, k)
        send(relay[buf], kvu[v].at[slot], ru.at[v, slot], dev(z, chip(side), k))

    def plane_u(v, step):
        hp = chip(step)
        slot = u_slot(2 * hp + k, k)
        arrived(kvu[v].at[slot], ru.at[v, slot])
        spread_u(v, hp, kvu[v].at[slot])

    def plane_4(v, step):
        side = relay_to[v][0]
        hp = chip(step)
        slot = 8 + 2 * hp + k
        arrived(kv4[v].at[slot], r4.at[v, slot])
        if step == 4 - side:
            send(kv4[v].at[slot], kv4[v].at[slot], r4.at[v, slot], dev(z, chip(side), k))
        spread_4(v, hp, kv4[v].at[slot])

    def planes(v, step):
        hp = chip(step)
        sign = 1 - 2 * lax.div(hp, 2)
        p = 2 * hp + k
        for q in (p - 8, p + 8):
            slot = u_slot(q, k)
            arrived(kvu[v].at[slot], ru.at[v, slot])
        far = lax.div(1 + sign, 2)
        target = u_slot(p + 16 * sign, far)
        send(
            kvu[v].at[u_slot(p + 8 * sign, k)], kvu[v].at[target], ru.at[v, target],
            dev(z - sign, h, far),
        )
        for q in (p - 8, p + 8):
            to = u_slot(q, other)
            send(kvu[v].at[u_slot(q, k)], kvu[v].at[to], ru.at[v, to], dev(z, h, other))
        for slot in (p, 16 + p):
            arrived(kv4[v].at[slot], r4.at[v, slot])
        if step == 2:
            send(
                kv4[v].at[8 + 8 * sign + p], kv4[v].at[24 + k], r4.at[v, 24 + k],
                dev(z - sign, h, k),
            )
        for slot in (p, 16 + p):
            send(kv4[v].at[slot], kv4[v].at[slot], r4.at[v, slot], dev(z, h, other))

    def pass_query():
        source = chip(3 - 2 * k)
        arrived(relay[2], rrelay.at[2])
        where = 2 * lax.rem(source, 2) + k
        send(
            relay[2], qu.at[where], rq.at[where],
            dev(z, lax.rem(source + 2, CHIPS), lax.div(source, 2)),
        )

    def mine_q(i):
        return jnp.logical_and(to_self, place_q == i)

    def biases_ready():
        frame_row = frames_ref[...][None, :]
        lane = lax.broadcasted_iota(jnp.int32, (1, 128), 1)
        rows = []
        for i in range(5):
            if i < 4:
                @pl.when(jnp.logical_not(mine_q(i)))
                def _():
                    arrived(adju.at[i], ra.at[i])
            shard = 8 * z + 4 * k + i if i < 4 else s_me
            for a in range(2):
                at = jnp.where(lane == 2 * shard + a, frame_row, -1)
                gap = jnp.abs(frame_row - jnp.max(at, axis=1, keepdims=True))
                linked = (adju[i, a : a + 1, :] if i < 4 else adj_ref[a : a + 1, :]) == 1
                fine = (gap == 0) | ((gap == 1) & linked)
                rows.append(jnp.where(fine, 0.0, BLOCKED))
        bias_v[...] = jnp.concatenate(rows + [jnp.zeros((6, 128), jnp.float32)], axis=0)

    def bias_copy():
        return pltpu.make_async_copy(bias_v, bias_s, bsem)

    def bias_of(i, first_shard, second_shard):
        found = [[], []]
        for shard in (first_shard, second_shard):
            valid = jnp.logical_and(shard >= 0, shard < 64)
            at = jnp.clip(shard, 0, 63)
            for a in range(2):
                for b in range(2):
                    found[a].append(jnp.where(valid, bias_s[2 * i + a, 2 * at + b], BLOCKED))
        return found

    def unit(n, carry):
        step = jnp.where(n < 3, 0, jnp.where(n < 5, 2 * n - 5, jnp.where(n < 7, 1, jnp.where(n < 9, 3, 2))))
        turn = jnp.where(n < 3, n, jnp.where(n < 5, 0, jnp.where(n < 7, n - 4, jnp.where(n < 9, n - 6, n - 9))))
        dz = jnp.where(turn == 0, 0, 2 * turn - 3)
        far = n >= 12
        p = 8 * dz + 2 * lax.rem(h + step, CHIPS)
        slot = jnp.where(far, 24 * k + 2 * (n - 12), u_slot(p, k))
        slot4 = jnp.where(far, 24 + 2 * (n - 12), 8 + p)
        shard = 8 * z + 4 * k + slot - 12
        side = jnp.where(h < 2, -2, 2)
        e0 = 8 * (z + side) + 2 * lax.rem(h + 2, CHIPS)
        e1 = jnp.where(h == 0, 8 * (z - 2) + 6, jnp.where(h == 3, 8 * (z + 2), -1000))
        shard4 = jnp.where(n < 12, 8 * z + p, jnp.where(n == 12, e0, e1))
        tiles = []
        keys = ku[pl.ds(slot, 2)].reshape(2 * TOK, HD)
        values = jnp.concatenate([vu[slot], vu[slot + 1]], axis=1)
        for i in range(4):
            tiles.append((i, qu[i], keys, values, bias_of(i, shard, shard + 1)))
        keys = k4[pl.ds(slot4, 2)].reshape(2 * TOK, HD)
        values = jnp.concatenate([v4[slot4], v4[slot4 + 1]], axis=1)
        tiles.append((4, qn[4], keys, values, bias_of(4, shard4, shard4 + 1)))
        fold(tiles, m_sc, l_sc, acc_sc)
        return carry

    def from_partner(dz, step):
        for v in range(2):
            slot = u_slot(8 * dz + 2 * chip(step) + other, k)
            arrived(kvu[v].at[slot], ru.at[v, slot])
            slot = 8 + 8 * dz + 2 * chip(step) + other
            arrived(kv4[v].at[slot], r4.at[v, slot])

    def compute(begin, end):
        lax.fori_loop(begin, end, unit, 0)

    pass_relay(0)
    plane_u(0, 3)
    plane_u(0, 1)
    plane_4(0, 3)
    plane_4(0, 1)
    planes(0, 0)
    planes(1, 0)
    biases_ready()
    planes(0, 1)
    planes(0, 3)
    plane_u(0, 2)
    plane_4(0, 2)
    bias_copy().start()
    pass_query()
    pass_relay(1)
    plane_u(1, 3)
    plane_u(1, 1)
    plane_4(1, 1)
    plane_4(1, 3)
    planes(0, 2)
    bias_copy().wait()
    for i in range(4):
        @pl.when(jnp.logical_not(mine_q(i)))
        def _():
            arrived(qu.at[i], rq.at[i])
    for dz in (0, -1, 1):
        from_partner(dz, 0)
    compute(0, 2)
    planes(1, 1)
    planes(1, 3)
    plane_u(1, 2)
    plane_4(1, 2)
    for step in (1, 3):
        from_partner(0, step)
    compute(2, 5)
    planes(1, 2)
    for step in (1, 3):
        from_partner(-1, step)
        from_partner(1, step)
    compute(5, 7)
    edge = lax.div(h, 2) * 3
    for v in range(2):
        e0, e1 = 24 + k, 26 + k
        arrived(kv4[v].at[e0], r4.at[v, e0])
        send(kv4[v].at[e0], kv4[v].at[e0], r4.at[v, e0], dev(z, h, other))
        send_if(inner, kv4[v].at[e0], kv4[v].at[e1], r4.at[v, e1], dev(z, edge, k))
    from_partner(0, 2)
    compute(7, 10)
    for v in range(2):
        e1 = 26 + k

        @pl.when(outer)
        def _():
            arrived(kv4[v].at[e1], r4.at[v, e1])

        send_if(outer, kv4[v].at[e1], kv4[v].at[e1], r4.at[v, e1], dev(z, h, other))
    from_partner(-1, 2)
    from_partner(1, 2)
    for v in range(2):
        for i in range(4):
            arrived(kvu[v].at[24 * k + i], ru.at[v, 24 * k + i])
        arrived(kv4[v].at[24 + other], r4.at[v, 24 + other])

        @pl.when(outer)
        def _():
            arrived(kv4[v].at[26 + other], r4.at[v, 26 + other])
    compute(10, 14)

    def give(i):
        hh, kk = 2 * k + i // 2, i % 2
        away = jnp.logical_not(jnp.logical_and(hh == h, kk == k))
        send_if(away, obuf.at[i], rbuf.at[h], ro.at[h], dev(z, hh, kk))

        @pl.when(jnp.logical_not(away))
        def _():
            rbuf[h] = obuf[i]

    for i in range(4):
        obuf[i] = (acc_sc[i] / l_sc[i]).T.astype(jnp.bfloat16)
        if i > 0:
            give(i - 1)
    out_ref[:, 4 * HD :] = (acc_sc[4] / l_sc[4]).T
    give(3)
    for step in (0, 1, 3, 2):
        head = chip(step)
        if step == 0:
            @pl.when(to_other)
            def _():
                arrived(rbuf.at[head], ro.at[head])
        else:
            arrived(rbuf.at[head], ro.at[head])
    for i in range(4):
        out_ref[:, i * HD : (i + 1) * HD] = rbuf[i].astype(jnp.float32)

    for copy, condition in sends:
        if condition is None:
            copy.wait_send()
        else:
            pl.when(condition)(copy.wait_send)


def shards(q_in, k_in, v_in, q_gain, k_gain, frames, adjacent):
    vmem = pl.BlockSpec(memory_space=pltpu.VMEM)
    bf16, f32, dma = jnp.bfloat16, jnp.float32, pltpu.SemaphoreType.DMA
    return pl.pallas_call(
        kernel,
        name="window_attention",
        out_shape=jax.ShapeDtypeStruct((TOK, HEADS * HD), f32),
        in_specs=[vmem] * 7,
        out_specs=vmem,
        scratch_shapes=[
            pltpu.VMEM((SLOTS, HD, TOK), bf16),
            pltpu.VMEM((SLOTS, TOK, HD), bf16),
            pltpu.VMEM((SLOTS, HD, TOK), bf16),
            pltpu.VMEM((SLOTS, TOK, HD), bf16),
            pltpu.VMEM((4, HD, TOK), bf16),
            pltpu.VMEM((4, 2, 128), jnp.int32),
            pltpu.VMEM((HEADS, HD, TOK), bf16),
            pltpu.VMEM((HEADS, TOK, HD), bf16),
            pltpu.VMEM((HEADS, HD, TOK), bf16),
            pltpu.VMEM((8, 128), f32),
            pltpu.VMEM((TENSOR, 8, 128), f32),
            pltpu.VMEM((HD, TOK), bf16),
            pltpu.VMEM((TOK, HD), bf16),
            pltpu.VMEM((HD, TOK), bf16),
            pltpu.VMEM((16, 128), f32),
            pltpu.SMEM((16, 128), f32),
            pltpu.VMEM((5, 1, TOK), f32),
            pltpu.VMEM((5, 1, TOK), f32),
            pltpu.VMEM((5, HD, TOK), f32),
            pltpu.VMEM((4, TOK, HD), bf16),
            pltpu.VMEM((4, TOK, HD), bf16),
            dma((160,)),
            dma,
            dma((2, SLOTS)),
            dma((2, SLOTS)),
            dma((4,)),
            dma((4,)),
            dma((3,)),
            dma((TENSOR,)),
            dma((4,)),
        ],
        compiler_params=pltpu.CompilerParams(collective_id=0, has_side_effects=True),
    )(q_in, k_in, v_in, q_gain, k_gain, adjacent, frames)


def solution(mesh):
    return jax.shard_map(
        shards,
        mesh=mesh,
        in_specs=(
            P("seq", "tensor"),
            P("seq", "tensor"),
            P("seq", "tensor"),
            P("tensor"),
            P("tensor"),
            P(),
            P("seq", None),
        ),
        out_specs=P("seq", "tensor"),
        check_vma=False,
    )
```

```python
import math

import jax
import jax.numpy as jnp
from jax import lax
from jax.experimental import pallas as pl
from jax.experimental.pallas import tpu as pltpu
from jax.sharding import PartitionSpec as P

HD = 128
TOK = 256
HEADS = 5
CHIPS = 4
PLANES = 8
TENSOR = 8
SLOTS = 36
COLUMN = 28
MESH = pl.DeviceIdType.MESH
EPS = 1e-06
BLOCKED = -1e30
EXP2_SCALE = math.log2(math.e) / math.sqrt(HD)


def place():
    s = lax.axis_index("seq")
    return lax.div(s, 8), lax.rem(lax.div(s, 2), 4), lax.rem(s, 2), lax.axis_index("tensor")


def fold(tiles, m_sc, l_sc, acc_sc):
    halves = (slice(0, 128), slice(128, 256))
    count = len(tiles)
    scores, weights, fades, sums = {}, {}, {}, {}

    def score(n):
        state, queries, keys, values, bias = tiles[n]
        scores[n] = jnp.dot(keys, queries, preferred_element_type=jnp.float32)

    def weigh(n):
        state, queries, keys, values, bias = tiles[n]
        s = scores.pop(n)
        blocks = s.shape[0] // 128
        columns, news, totals = [], [], []
        for a in range(2):
            new = m_sc[state, :, halves[a]]
            for b in range(blocks):
                top = jnp.max(s[b * 128 : (b + 1) * 128, halves[a]], axis=0, keepdims=True)
                new = jnp.maximum(new, top * EXP2_SCALE + bias[a][b])
            parts = [
                jnp.exp2(s[b * 128 : (b + 1) * 128, halves[a]] * EXP2_SCALE - (new - bias[a][b]))
                for b in range(blocks)
            ]
            column = jnp.concatenate(parts, axis=0)
            totals.append(jnp.sum(column, axis=0, keepdims=True))
            columns.append(column.astype(jnp.bfloat16))
            news.append(new)
        new = jnp.concatenate(news, axis=1)
        fades[n] = jnp.exp2(m_sc[state] - new)
        m_sc[state] = new
        l_sc[state] = l_sc[state] * fades[n] + jnp.concatenate(totals, axis=1)
        weights[n] = jnp.concatenate(columns, axis=1)

    def mix(n):
        state, queries, keys, values, bias = tiles[n]
        mixed = jnp.dot(values, weights.pop(n), preferred_element_type=jnp.float32)
        acc_sc[state] = acc_sc[state] * fades.pop(n) + mixed

    score(0)
    for n in range(count):
        if n + 1 < count:
            score(n + 1)
        if n > 0:
            mix(n - 1)
        weigh(n)
    mix(count - 1)


def kernel(
    q_ref, k_ref, v_ref, qg_ref, kg_ref, adj_ref, frames_ref,
    out_ref,
    vs, ks, qs, adju, qn, kn, vt, stat, statr,
    bias_v, bias_s, m_sc, l_sc, acc_sc, obuf, rbuf, obuf4, rbuf4, ost, rst,
    ssem, bsem, rkv, rq, ra, rstat, ro, ro4, rost,
):
    z, h, k, t = place()
    other = 1 - k
    kv = (vs, ks)
    s_me = lax.axis_index("seq")
    upper = lax.div(h, 2)
    far_core = 1 - upper
    is_far = k == far_core

    def dev(zz, hh, kk):
        return (lax.rem(zz + PLANES, PLANES) * 8 + hh * 2 + kk, t)

    def chip(step):
        return lax.rem(h + step, CHIPS)

    sends = []

    def send(src, dst, rsem, device, condition=None):
        copy = pltpu.make_async_remote_copy(
            src_ref=src, dst_ref=dst, send_sem=ssem.at[len(sends)], recv_sem=rsem,
            device_id=device, device_id_type=MESH,
        )
        sends.append((copy, condition))
        if condition is None:
            copy.start()
        else:
            pl.when(condition)(copy.start)

    def send_kv(v, src, slot, device):
        send(src, kv[v].at[slot], rkv.at[v, slot], device)

    def arrived(dst, rsem):
        pltpu.make_async_copy(dst, dst, rsem).wait()

    def arrived_kv(v, slot):
        arrived(kv[v].at[slot], rkv.at[v, slot])

    barrier = pltpu.get_barrier_semaphore()
    peers = [dev(z, h, other)]
    for step in (1, 2, 3):
        peers += [dev(z, chip(step), 0), dev(z, chip(step), 1)]
    for zz in (z + 1, z - 1):
        peers += [dev(zz, h, 0), dev(zz, h, 1)]
    for step in range(1, TENSOR):
        peers.append((s_me, lax.rem(t + step, TENSOR)))
    for peer in peers:
        pl.semaphore_signal(barrier, inc=1, device_id=peer, device_id_type=MESH)

    eye = lax.broadcasted_iota(jnp.int32, (128, 128), 0) == lax.broadcasted_iota(
        jnp.int32, (128, 128), 1
    )
    rows = []
    for ref in (q_ref, k_ref):
        for half in range(2):
            part = ref[half * 128 : (half + 1) * 128, :]
            column = jnp.sum(part * part, axis=1, keepdims=True)
            rows.append(jnp.sum(jnp.where(eye, column, 0.0), axis=0, keepdims=True))
    mine = jnp.concatenate(rows + [jnp.zeros((4, 128), jnp.float32)], axis=0)
    stat[...] = mine
    statr[t] = mine

    def u_slot(position, core):
        return position + 12 - 4 * core

    own = 2 * h + k
    for i in range(HEADS):
        vt[i] = v_ref[:, i * HD : (i + 1) * HD].T
    vs[u_slot(own, k)] = vt[h]
    vs[COLUMN + 2 + k] = vt[4]
    m_sc[...] = jnp.full_like(m_sc, -1e29)
    l_sc[...] = jnp.zeros_like(l_sc)
    acc_sc[...] = jnp.zeros_like(acc_sc)

    pl.semaphore_wait(barrier, len(peers))

    for step in range(1, TENSOR):
        send(stat, statr.at[t], rstat.at[t], (s_me, lax.rem(t + step, TENSOR)))

    def spread_u(v, hp, src):
        p = 2 * hp + k
        send_kv(v, src, u_slot(p - 8, k), dev(z + 1, h, k))
        send_kv(v, src, u_slot(p + 8, k), dev(z - 1, h, k))
        send_kv(v, src, u_slot(p, other), dev(z, h, other))

    def first(v, ref):
        for step in (2, 1, 3):
            send_kv(v, ref.at[chip(step)], u_slot(own, k), dev(z, chip(step), k))
        spread_u(v, h, ref.at[h])
        send_kv(v, ref.at[4], COLUMN + k, dev(z + 1, h, k))
        send_kv(v, ref.at[4], COLUMN + 4 + k, dev(z - 1, h, k))
        send_kv(v, ref.at[4], COLUMN + 2 + k, dev(z, h, other))

    first(0, vt)

    core = upper
    place_q = 2 * lax.rem(h, 2) + k
    to_self = core == k
    to_other = jnp.logical_not(to_self)
    for step in (1, 2, 3):
        send(adj_ref, adju.at[place_q], ra.at[place_q], dev(z, chip(step), core))
    send(adj_ref, adju.at[place_q], ra.at[place_q], dev(z, h, other), to_other)

    for step in range(1, TENSOR):
        j = lax.rem(t + step, TENSOR)
        arrived(statr.at[j], rstat.at[j])
    total = statr[0]
    for j in range(1, TENSOR):
        total = total + statr[j]
    inverse = 1.0 / jnp.sqrt(total / float(HD * HEADS * TENSOR) + EPS)

    def normalize(row, half, ref, gain, put):
        lane_row = inverse[row + half : row + half + 1, :]
        column = jnp.sum(jnp.where(eye, lane_row, 0.0), axis=1, keepdims=True)
        span = slice(half * 128, (half + 1) * 128)
        for i in range(HEADS):
            feature = slice(i * HD, (i + 1) * HD)
            put(i, span, ref[span, feature] * column * gain[feature][None, :])

    def put_k(i, span, x):
        kn[i, span, :] = x.astype(jnp.bfloat16)

    def put_q(i, span, x):
        qn[i, :, span] = x.T.astype(jnp.bfloat16)

    normalize(2, 0, k_ref, kg_ref, put_k)
    normalize(2, 1, k_ref, kg_ref, put_k)
    normalize(0, 0, q_ref, qg_ref, put_q)
    first(1, kn)
    ks[u_slot(own, k)] = kn[h]
    ks[COLUMN + 2 + k] = kn[4]
    normalize(0, 1, q_ref, qg_ref, put_q)

    @pl.when(to_self)
    def _():
        qs[place_q] = qn[h]
        qs[4 + place_q] = qn[4]
        adju[place_q] = adj_ref[...]

    for base, head in ((0, chip), (4, lambda step: 4)):
        at = base + place_q
        for step in (2, 1, 3):
            send(qn.at[head(step)], qs.at[at], rq.at[at], dev(z, chip(step), core))
        send(qn.at[head(0)], qs.at[at], rq.at[at], dev(z, h, other), to_other)

    def plane_u(v, step):
        slot = u_slot(2 * chip(step) + k, k)
        arrived_kv(v, slot)
        spread_u(v, chip(step), kv[v].at[slot])

    def planes_u(v, step):
        hp = chip(step)
        sign = 1 - 2 * lax.div(hp, 2)
        p = 2 * hp + k
        for q in (p - 8, p + 8):
            arrived_kv(v, u_slot(q, k))
        far = lax.div(1 + sign, 2)
        send_kv(
            v, kv[v].at[u_slot(p + 8 * sign, k)], u_slot(p + 16 * sign, far),
            dev(z - sign, h, far),
        )
        for q in (p - 8, p + 8):
            send_kv(v, kv[v].at[u_slot(q, k)], u_slot(q, other), dev(z, h, other))

    def planes_4(v):
        low, high = COLUMN + k, COLUMN + 4 + k
        arrived_kv(v, low)
        arrived_kv(v, high)
        send_kv(
            v, kv[v].at[COLUMN + 4 * far_core + k], COLUMN + 6 + k,
            dev(z + 2 * upper - 1, h, far_core),
        )
        for slot in (low, high):
            send_kv(v, kv[v].at[slot], slot, dev(z, h, other))

    def mine_q(i):
        return jnp.logical_and(to_self, place_q == i)

    def unless_mine(i, wait):
        pl.when(jnp.logical_not(mine_q(i)))(wait)

    def biases_ready():
        frame_row = frames_ref[...][None, :]
        lane = lax.broadcasted_iota(jnp.int32, (1, 128), 1)
        rows = []
        for i in range(4):
            unless_mine(i, lambda: arrived(adju.at[i], ra.at[i]))
            shard = 8 * z + 4 * k + i
            for a in range(2):
                at = jnp.where(lane == 2 * shard + a, frame_row, -1)
                gap = jnp.abs(frame_row - jnp.max(at, axis=1, keepdims=True))
                fine = (gap == 0) | ((gap == 1) & (adju[i, a : a + 1, :] == 1))
                rows.append(jnp.where(fine, 0.0, BLOCKED))
        bias_v[...] = jnp.concatenate(rows, axis=0)

    def bias_copy():
        return pltpu.make_async_copy(bias_v, bias_s, bsem)

    def bias_of(i, first_shard):
        found = [[], []]
        for shard in (first_shard, first_shard + 1):
            valid = jnp.logical_and(shard >= 0, shard < 64)
            at = jnp.clip(shard, 0, 63)
            for a in range(2):
                for b in range(2):
                    found[a].append(jnp.where(valid, bias_s[2 * i + a, 2 * at + b], BLOCKED))
        return found

    def unit(n, carry):
        step = jnp.where(
            n < 3, 0, jnp.where(n < 5, 2 * n - 5, jnp.where(n < 7, 1, jnp.where(n < 9, 3, 2)))
        )
        turn = jnp.where(
            n < 3, n, jnp.where(n < 5, 0, jnp.where(n < 7, n - 4, jnp.where(n < 9, n - 6, n - 9)))
        )
        dz = jnp.where(turn == 0, 0, 2 * turn - 3)
        slot = jnp.where(
            n >= 12, 24 * k + 2 * (n - 12), u_slot(8 * dz + 2 * lax.rem(h + step, CHIPS), k)
        )
        shard = 8 * z + 4 * k + slot - 12
        turn4 = n - 14
        dz4 = jnp.where(turn4 == 3, 2 - 4 * upper, jnp.where(turn4 == 0, 0, 2 * turn4 - 3))
        slot4 = COLUMN + jnp.where(turn4 == 0, 2, jnp.where(turn4 == 1, 0, 2 * turn4))
        column = n >= 14
        slot = jnp.where(column, slot4, slot)
        shard = jnp.where(column, 8 * (z + dz4) + 2 * h, shard)
        base = jnp.where(column, 4, 0)
        keys = ks[pl.ds(slot, 2)].reshape(2 * TOK, HD)
        values = jnp.concatenate([vs[slot], vs[slot + 1]], axis=1)
        fold(
            [(base + i, qs[base + i], keys, values, bias_of(i, shard)) for i in range(4)],
            m_sc, l_sc, acc_sc,
        )
        return carry

    def from_partner(dz, step):
        for v in range(2):
            arrived_kv(v, u_slot(8 * dz + 2 * chip(step) + other, k))

    def compute(begin, end):
        lax.fori_loop(begin, end, unit, 0)

    planes_u(0, 0)
    planes_4(0)
    plane_u(0, 1)
    plane_u(0, 3)
    plane_u(0, 2)
    biases_ready()
    planes_u(1, 0)
    planes_4(1)
    planes_u(0, 1)
    planes_u(0, 3)
    plane_u(1, 1)
    plane_u(1, 3)
    bias_copy().start()
    planes_u(0, 2)
    plane_u(1, 2)
    planes_u(1, 1)
    planes_u(1, 3)
    bias_copy().wait()
    for i in range(4):
        unless_mine(i, lambda: arrived(qs.at[i], rq.at[i]))
    for dz in (0, -1, 1):
        from_partner(dz, 0)
    compute(0, 3)
    planes_u(1, 2)
    for step in (1, 3):
        from_partner(0, step)
        from_partner(-1, step)
        from_partner(1, step)
    compute(3, 9)

    for i in range(4):
        unless_mine(i, lambda: arrived(qs.at[4 + i], rq.at[4 + i]))
    for v in range(2):
        for slot in (0, 2, 4):
            arrived_kv(v, COLUMN + slot + other)

        @pl.when(is_far)
        def _():
            arrived_kv(v, COLUMN + 6)
            arrived_kv(v, COLUMN + 7)

    compute(14, jnp.where(is_far, 18, 17))
    for i in range(4):
        total = l_sc[4 + i]
        obuf4[i] = (acc_sc[4 + i] / jnp.maximum(total, 1e-30)).astype(jnp.bfloat16)
        ost[i] = jnp.concatenate([m_sc[4 + i], total], axis=0)

    def owner(i):
        return 2 * k + i // 2, i % 2

    def away(i):
        hh, kk = owner(i)
        return jnp.logical_not(jnp.logical_and(hh == h, kk == k))

    def give(i, src, dst, rsem):
        send(src.at[i], dst.at[h], rsem.at[h], dev(z, *owner(i)), away(i))

        @pl.when(jnp.logical_not(away(i)))
        def _():
            dst[h] = src[i]

    from_partner(0, 2)
    from_partner(-1, 2)
    from_partner(1, 2)
    for v in range(2):
        for i in range(4):
            arrived_kv(v, 24 * k + i)
    for i in range(4):
        give(i, obuf4, rbuf4, ro4)
        give(i, ost, rst, rost)
    compute(9, 14)

    for i in range(4):
        obuf[i] = (acc_sc[i] / l_sc[i]).T.astype(jnp.bfloat16)
        if i > 0:
            give(i - 1, obuf, rbuf, ro)

    def returned(head, dst, rsem):
        pl.when(jnp.logical_not(jnp.logical_and(to_self, head == h)))(
            lambda: arrived(dst.at[head], rsem.at[head])
        )

    for head in range(4):
        returned(head, rbuf4, ro4)
        returned(head, rst, rost)
    give(3, obuf, rbuf, ro)
    top = jnp.maximum(
        jnp.maximum(rst[0, 0:1], rst[1, 0:1]), jnp.maximum(rst[2, 0:1], rst[3, 0:1])
    )
    shares = [rst[j, 1:2] * jnp.exp2(rst[j, 0:1] - top) for j in range(4)]
    whole = shares[0] + shares[1] + shares[2] + shares[3]
    merged = rbuf4[0].astype(jnp.float32) * shares[0]
    for j in range(1, 4):
        merged = merged + rbuf4[j].astype(jnp.float32) * shares[j]
    out_ref[:, 4 * HD :] = (merged / whole).T
    for head in range(4):
        returned(head, rbuf, ro)
    for head in range(4):
        out_ref[:, head * HD : (head + 1) * HD] = rbuf[head].astype(jnp.float32)

    for copy, condition in sends:
        if condition is None:
            copy.wait_send()
        else:
            pl.when(condition)(copy.wait_send)


def shards(q_in, k_in, v_in, q_gain, k_gain, frames, adjacent):
    vmem = pl.BlockSpec(memory_space=pltpu.VMEM)
    bf16, f32, dma = jnp.bfloat16, jnp.float32, pltpu.SemaphoreType.DMA
    return pl.pallas_call(
        kernel,
        name="window_attention",
        out_shape=jax.ShapeDtypeStruct((TOK, HEADS * HD), f32),
        in_specs=[vmem] * 7,
        out_specs=vmem,
        scratch_shapes=[
            pltpu.VMEM((SLOTS, HD, TOK), bf16),
            pltpu.VMEM((SLOTS, TOK, HD), bf16),
            pltpu.VMEM((8, HD, TOK), bf16),
            pltpu.VMEM((4, 2, 128), jnp.int32),
            pltpu.VMEM((HEADS, HD, TOK), bf16),
            pltpu.VMEM((HEADS, TOK, HD), bf16),
            pltpu.VMEM((HEADS, HD, TOK), bf16),
            pltpu.VMEM((8, 128), f32),
            pltpu.VMEM((TENSOR, 8, 128), f32),
            pltpu.VMEM((8, 128), f32),
            pltpu.SMEM((8, 128), f32),
            pltpu.VMEM((8, 1, TOK), f32),
            pltpu.VMEM((8, 1, TOK), f32),
            pltpu.VMEM((8, HD, TOK), f32),
            pltpu.VMEM((4, TOK, HD), bf16),
            pltpu.VMEM((4, TOK, HD), bf16),
            pltpu.VMEM((4, HD, TOK), bf16),
            pltpu.VMEM((4, HD, TOK), bf16),
            pltpu.VMEM((4, 2, TOK), f32),
            pltpu.VMEM((4, 2, TOK), f32),
            dma((128,)),
            dma,
            dma((2, SLOTS)),
            dma((8,)),
            dma((4,)),
            dma((TENSOR,)),
            dma((4,)),
            dma((4,)),
            dma((4,)),
        ],
        compiler_params=pltpu.CompilerParams(collective_id=0, has_side_effects=True),
    )(q_in, k_in, v_in, q_gain, k_gain, adjacent, frames)


def solution(mesh):
    return jax.shard_map(
        shards,
        mesh=mesh,
        in_specs=(
            P("seq", "tensor"),
            P("seq", "tensor"),
            P("seq", "tensor"),
            P("tensor"),
            P("tensor"),
            P(),
            P("seq", None),
        ),
        out_specs=P("seq", "tensor"),
        check_vma=False,
    )
```

```python
import math

import jax
import jax.numpy as jnp
from jax import lax
from jax.experimental import pallas as pl
from jax.experimental.pallas import tpu as pltpu
from jax.sharding import PartitionSpec as P

HD = 128
TOK = 256
HEADS = 5
CHIPS = 4
PLANES = 8
TENSOR = 8
SLOTS = 36
COLUMN = 28
MESH = pl.DeviceIdType.MESH
EPS = 1e-06
BLOCKED = -1e30
EXP2_SCALE = math.log2(math.e) / math.sqrt(HD)


def place():
    s = lax.axis_index("seq")
    return lax.div(s, 8), lax.rem(lax.div(s, 2), 4), lax.rem(s, 2), lax.axis_index("tensor")


def fold(tiles, m_sc, l_sc, acc_sc):
    halves = (slice(0, 128), slice(128, 256))
    count = len(tiles)
    scores, weights, fades, sums = {}, {}, {}, {}

    def score(n):
        state, queries, keys, values, bias = tiles[n]
        scores[n] = jnp.dot(keys, queries, preferred_element_type=jnp.float32)

    def weigh(n):
        state, queries, keys, values, bias = tiles[n]
        s = scores.pop(n)
        blocks = s.shape[0] // 128
        columns, news, totals = [], [], []
        for a in range(2):
            new = m_sc[state, :, halves[a]]
            for b in range(blocks):
                top = jnp.max(s[b * 128 : (b + 1) * 128, halves[a]], axis=0, keepdims=True)
                new = jnp.maximum(new, top * EXP2_SCALE + bias[a][b])
            parts = [
                jnp.exp2(s[b * 128 : (b + 1) * 128, halves[a]] * EXP2_SCALE - (new - bias[a][b]))
                for b in range(blocks)
            ]
            column = jnp.concatenate(parts, axis=0)
            totals.append(jnp.sum(column, axis=0, keepdims=True))
            columns.append(column.astype(jnp.bfloat16))
            news.append(new)
        new = jnp.concatenate(news, axis=1)
        fades[n] = jnp.exp2(m_sc[state] - new)
        m_sc[state] = new
        l_sc[state] = l_sc[state] * fades[n] + jnp.concatenate(totals, axis=1)
        weights[n] = jnp.concatenate(columns, axis=1)

    def mix(n):
        state, queries, keys, values, bias = tiles[n]
        mixed = jnp.dot(values, weights.pop(n), preferred_element_type=jnp.float32)
        acc_sc[state] = acc_sc[state] * fades.pop(n) + mixed

    score(0)
    for n in range(count):
        if n + 1 < count:
            score(n + 1)
        if n > 0:
            mix(n - 1)
        weigh(n)
    mix(count - 1)


def kernel(
    q_hbm, k_hbm, v_hbm, qg_ref, kg_ref, adj_ref, frames_ref,
    out_ref,
    q_ref, k_ref, v_ref,
    vs, ks, qs, adju, qn, kn, vt, stat, statr,
    bias_v, bias_s, m_sc, l_sc, acc_sc, obuf, rbuf, obuf4, rbuf4, ost, rst,
    ssem, bsem, isem, rkv, rq, ra, rstat, ro, ro4, rost,
):
    z, h, k, t = place()
    other = 1 - k
    kv = (vs, ks)
    s_me = lax.axis_index("seq")
    upper = lax.div(h, 2)
    far_core = 1 - upper
    is_far = k == far_core

    def dev(zz, hh, kk):
        return (lax.rem(zz + PLANES, PLANES) * 8 + hh * 2 + kk, t)

    def chip(step):
        return lax.rem(h + step, CHIPS)

    sends = []

    def send(src, dst, rsem, device, condition=None):
        copy = pltpu.make_async_remote_copy(
            src_ref=src, dst_ref=dst, send_sem=ssem.at[len(sends)], recv_sem=rsem,
            device_id=device, device_id_type=MESH,
        )
        sends.append((copy, condition))
        if condition is None:
            copy.start()
        else:
            pl.when(condition)(copy.start)

    def send_kv(v, src, slot, device):
        send(src, kv[v].at[slot], rkv.at[v, slot], device)

    def arrived(dst, rsem):
        pltpu.make_async_copy(dst, dst, rsem).wait()

    def arrived_kv(v, slot):
        arrived(kv[v].at[slot], rkv.at[v, slot])

    loads = [
        pltpu.make_async_copy(src, dst, isem.at[n])
        for n, (src, dst) in enumerate(((q_hbm, q_ref), (k_hbm, k_ref), (v_hbm, v_ref)))
    ]
    for load in loads:
        load.start()

    barrier = pltpu.get_barrier_semaphore()
    peers = [dev(z, h, other)]
    for step in (1, 2, 3):
        peers += [dev(z, chip(step), 0), dev(z, chip(step), 1)]
    for zz in (z + 1, z - 1):
        peers += [dev(zz, h, 0), dev(zz, h, 1)]
    for step in range(1, TENSOR):
        peers.append((s_me, lax.rem(t + step, TENSOR)))
    for peer in peers:
        pl.semaphore_signal(barrier, inc=1, device_id=peer, device_id_type=MESH)

    for load in loads:
        load.wait()

    eye = lax.broadcasted_iota(jnp.int32, (128, 128), 0) == lax.broadcasted_iota(
        jnp.int32, (128, 128), 1
    )
    rows = []
    for ref in (q_ref, k_ref):
        for half in range(2):
            part = ref[half * 128 : (half + 1) * 128, :]
            column = jnp.sum(part * part, axis=1, keepdims=True)
            rows.append(jnp.sum(jnp.where(eye, column, 0.0), axis=0, keepdims=True))
    mine = jnp.concatenate(rows + [jnp.zeros((4, 128), jnp.float32)], axis=0)
    stat[...] = mine
    statr[t] = mine

    def u_slot(position, core):
        return position + 12 - 4 * core

    own = 2 * h + k
    for i in range(HEADS):
        vt[i] = v_ref[:, i * HD : (i + 1) * HD].T
    vs[u_slot(own, k)] = vt[h]
    vs[COLUMN + 2 + k] = vt[4]
    m_sc[...] = jnp.full_like(m_sc, -1e29)
    l_sc[...] = jnp.zeros_like(l_sc)
    acc_sc[...] = jnp.zeros_like(acc_sc)

    pl.semaphore_wait(barrier, len(peers))

    for step in range(1, TENSOR):
        send(stat, statr.at[t], rstat.at[t], (s_me, lax.rem(t + step, TENSOR)))

    def spread_u(v, hp, src):
        p = 2 * hp + k
        send_kv(v, src, u_slot(p - 8, k), dev(z + 1, h, k))
        send_kv(v, src, u_slot(p + 8, k), dev(z - 1, h, k))
        send_kv(v, src, u_slot(p, other), dev(z, h, other))

    def first_y(v, ref, steps):
        for step in steps:
            send_kv(v, ref.at[chip(step)], u_slot(own, k), dev(z, chip(step), k))

    def first_z(v, ref):
        spread_u(v, h, ref.at[h])
        send_kv(v, ref.at[4], COLUMN + k, dev(z + 1, h, k))
        send_kv(v, ref.at[4], COLUMN + 4 + k, dev(z - 1, h, k))
        send_kv(v, ref.at[4], COLUMN + 2 + k, dev(z, h, other))

    first_y(0, vt, (2, 1, 3))
    first_z(0, vt)

    core = upper
    place_q = 2 * lax.rem(h, 2) + k
    to_self = core == k
    to_other = jnp.logical_not(to_self)
    for step in (1, 2, 3):
        send(adj_ref, adju.at[place_q], ra.at[place_q], dev(z, chip(step), core))
    send(adj_ref, adju.at[place_q], ra.at[place_q], dev(z, h, other), to_other)

    for step in range(1, TENSOR):
        j = lax.rem(t + step, TENSOR)
        arrived(statr.at[j], rstat.at[j])
    total = statr[0]
    for j in range(1, TENSOR):
        total = total + statr[j]
    inverse = 1.0 / jnp.sqrt(total / float(HD * HEADS * TENSOR) + EPS)

    def normalize(row, half, ref, gain, put):
        lane_row = inverse[row + half : row + half + 1, :]
        column = jnp.sum(jnp.where(eye, lane_row, 0.0), axis=1, keepdims=True)
        span = slice(half * 128, (half + 1) * 128)
        for i in range(HEADS):
            feature = slice(i * HD, (i + 1) * HD)
            put(i, span, ref[span, feature] * column * gain[feature][None, :])

    def put_k(i, span, x):
        kn[i, span, :] = x.astype(jnp.bfloat16)

    def put_q(i, span, x):
        qn[i, :, span] = x.T.astype(jnp.bfloat16)

    normalize(2, 0, k_ref, kg_ref, put_k)
    normalize(2, 1, k_ref, kg_ref, put_k)
    normalize(0, 0, q_ref, qg_ref, put_q)
    first_z(1, kn)
    ks[u_slot(own, k)] = kn[h]
    ks[COLUMN + 2 + k] = kn[4]
    normalize(0, 1, q_ref, qg_ref, put_q)

    @pl.when(to_self)
    def _():
        qs[place_q] = qn[h]
        qs[4 + place_q] = qn[4]
        adju[place_q] = adj_ref[...]

    for base, head in ((0, chip), (4, lambda step: 4)):
        at = base + place_q
        for step in (2, 1, 3):
            send(qn.at[head(step)], qs.at[at], rq.at[at], dev(z, chip(step), core))
        send(qn.at[head(0)], qs.at[at], rq.at[at], dev(z, h, other), to_other)
    first_y(1, kn, (1, 3, 2))

    def plane_u(v, step):
        slot = u_slot(2 * chip(step) + k, k)
        arrived_kv(v, slot)
        spread_u(v, chip(step), kv[v].at[slot])

    def planes_u(v, step):
        hp = chip(step)
        sign = 1 - 2 * lax.div(hp, 2)
        p = 2 * hp + k
        for q in (p - 8, p + 8):
            arrived_kv(v, u_slot(q, k))
        far = lax.div(1 + sign, 2)
        send_kv(
            v, kv[v].at[u_slot(p + 8 * sign, k)], u_slot(p + 16 * sign, far),
            dev(z - sign, h, far),
        )
        for q in (p - 8, p + 8):
            send_kv(v, kv[v].at[u_slot(q, k)], u_slot(q, other), dev(z, h, other))

    def planes_4(v):
        low, high = COLUMN + k, COLUMN + 4 + k
        arrived_kv(v, low)
        arrived_kv(v, high)
        send_kv(
            v, kv[v].at[COLUMN + 4 * far_core + k], COLUMN + 6 + k,
            dev(z + 2 * upper - 1, h, far_core),
        )
        for slot in (low, high):
            send_kv(v, kv[v].at[slot], slot, dev(z, h, other))

    def mine_q(i):
        return jnp.logical_and(to_self, place_q == i)

    def unless_mine(i, wait):
        pl.when(jnp.logical_not(mine_q(i)))(wait)

    def biases_ready():
        frame_row = frames_ref[...][None, :]
        lane = lax.broadcasted_iota(jnp.int32, (1, 128), 1)
        rows = []
        for i in range(4):
            unless_mine(i, lambda: arrived(adju.at[i], ra.at[i]))
            shard = 8 * z + 4 * k + i
            for a in range(2):
                at = jnp.where(lane == 2 * shard + a, frame_row, -1)
                gap = jnp.abs(frame_row - jnp.max(at, axis=1, keepdims=True))
                fine = (gap == 0) | ((gap == 1) & (adju[i, a : a + 1, :] == 1))
                rows.append(jnp.where(fine, 0.0, BLOCKED))
        bias_v[...] = jnp.concatenate(rows, axis=0)

    def bias_copy():
        return pltpu.make_async_copy(bias_v, bias_s, bsem)

    def bias_of(i, first_shard):
        found = [[], []]
        for shard in (first_shard, first_shard + 1):
            valid = jnp.logical_and(shard >= 0, shard < 64)
            at = jnp.clip(shard, 0, 63)
            for a in range(2):
                for b in range(2):
                    found[a].append(jnp.where(valid, bias_s[2 * i + a, 2 * at + b], BLOCKED))
        return found

    def keys_of(n):
        step = jnp.where(
            n < 3, 0, jnp.where(n < 5, 2 * n - 5, jnp.where(n < 7, 1, jnp.where(n < 9, 3, 2)))
        )
        turn = jnp.where(
            n < 3, n, jnp.where(n < 5, 0, jnp.where(n < 7, n - 4, jnp.where(n < 9, n - 6, n - 9)))
        )
        dz = jnp.where(turn == 0, 0, 2 * turn - 3)
        slot = jnp.where(
            n >= 12, 24 * k + 2 * (n - 12), u_slot(8 * dz + 2 * lax.rem(h + step, CHIPS), k)
        )
        shard = 8 * z + 4 * k + slot - 12
        turn4 = n - 14
        dz4 = jnp.where(turn4 == 3, 2 - 4 * upper, jnp.where(turn4 == 0, 0, 2 * turn4 - 3))
        slot4 = COLUMN + jnp.where(turn4 == 0, 2, jnp.where(turn4 == 1, 0, 2 * turn4))
        column = n >= 14
        slot = jnp.where(column, slot4, slot)
        shard = jnp.where(column, 8 * (z + dz4) + 2 * h, shard)
        keys = ks[pl.ds(slot, 2)].reshape(2 * TOK, HD)
        values = jnp.concatenate([vs[slot], vs[slot + 1]], axis=1)
        return keys, values, shard, jnp.where(column, 4, 0)

    def unit(n, carry):
        keys, values, shard, base = keys_of(n)
        fold(
            [(base + i, qs[base + i], keys, values, bias_of(i, shard)) for i in range(4)],
            m_sc, l_sc, acc_sc,
        )
        return carry

    def last_units(low):
        def pair(j, carry):
            tiles = []
            for n in (10 + 2 * j, 11 + 2 * j):
                keys, values, shard, _ = keys_of(n)
                for i in (low, low + 1):
                    tiles.append((i, qs[i], keys, values, bias_of(i, shard)))
            fold(tiles, m_sc, l_sc, acc_sc)
            return carry

        lax.fori_loop(0, 2, pair, 0)

    def from_partner(dz, step):
        for v in range(2):
            arrived_kv(v, u_slot(8 * dz + 2 * chip(step) + other, k))

    def compute(begin, end):
        lax.fori_loop(begin, end, unit, 0)

    def owner(i):
        return 2 * k + i // 2, i % 2

    def away(i):
        hh, kk = owner(i)
        return jnp.logical_not(jnp.logical_and(hh == h, kk == k))

    def give(i, src, dst, rsem):
        send(src.at[i], dst.at[h], rsem.at[h], dev(z, *owner(i)), away(i))

        @pl.when(jnp.logical_not(away(i)))
        def _():
            dst[h] = src[i]

    planes_u(0, 0)
    planes_4(0)
    plane_u(0, 1)
    plane_u(0, 3)
    plane_u(0, 2)
    biases_ready()
    planes_u(1, 0)
    planes_4(1)
    planes_u(0, 1)
    planes_u(0, 3)
    bias_copy().start()
    planes_u(0, 2)
    bias_copy().wait()
    for i in range(4):
        unless_mine(i, lambda: arrived(qs.at[i], rq.at[i]))
    for dz in (0, -1, 1):
        from_partner(dz, 0)
    compute(0, 3)

    for i in range(4):
        unless_mine(i, lambda: arrived(qs.at[4 + i], rq.at[4 + i]))
    for v in range(2):
        for slot in (0, 2, 4):
            arrived_kv(v, COLUMN + slot + other)

        @pl.when(is_far)
        def _():
            arrived_kv(v, COLUMN + 6)
            arrived_kv(v, COLUMN + 7)

    compute(14, 16)
    plane_u(1, 1)
    plane_u(1, 3)
    compute(16, jnp.where(is_far, 18, 17))
    for i in range(4):
        total = l_sc[4 + i]
        obuf4[i] = (acc_sc[4 + i] / jnp.maximum(total, 1e-30)).astype(jnp.bfloat16)
        ost[i] = jnp.concatenate([m_sc[4 + i], total], axis=0)
    plane_u(1, 2)
    for i in range(4):
        give(i, obuf4, rbuf4, ro4)
        give(i, ost, rst, rost)
    planes_u(1, 1)
    planes_u(1, 3)
    for step in (1, 3):
        from_partner(0, step)
    compute(3, 5)
    planes_u(1, 2)
    for step in (1, 3):
        from_partner(-1, step)
        from_partner(1, step)
    compute(5, 9)
    from_partner(0, 2)
    from_partner(-1, 2)
    from_partner(1, 2)
    for v in range(2):
        for i in range(4):
            arrived_kv(v, 24 * k + i)
    compute(9, 10)

    for low in (0, 2):
        last_units(low)
        for i in (low, low + 1):
            obuf[i] = (acc_sc[i] / l_sc[i]).T.astype(jnp.bfloat16)
        for i in (low, low + 1):
            give(i, obuf, rbuf, ro)

    def returned(head, dst, rsem):
        pl.when(jnp.logical_not(jnp.logical_and(to_self, head == h)))(
            lambda: arrived(dst.at[head], rsem.at[head])
        )

    for head in range(4):
        returned(head, rbuf4, ro4)
        returned(head, rst, rost)
    top = jnp.maximum(
        jnp.maximum(rst[0, 0:1], rst[1, 0:1]), jnp.maximum(rst[2, 0:1], rst[3, 0:1])
    )
    shares = [rst[j, 1:2] * jnp.exp2(rst[j, 0:1] - top) for j in range(4)]
    whole = shares[0] + shares[1] + shares[2] + shares[3]
    merged = rbuf4[0].astype(jnp.float32) * shares[0]
    for j in range(1, 4):
        merged = merged + rbuf4[j].astype(jnp.float32) * shares[j]
    out_ref[:, 4 * HD :] = (merged / whole).T
    for head in range(4):
        returned(head, rbuf, ro)
    for head in range(4):
        out_ref[:, head * HD : (head + 1) * HD] = rbuf[head].astype(jnp.float32)

    for copy, condition in sends:
        if condition is None:
            copy.wait_send()
        else:
            pl.when(condition)(copy.wait_send)


def shards(q_in, k_in, v_in, q_gain, k_gain, frames, adjacent):
    vmem = pl.BlockSpec(memory_space=pltpu.VMEM)
    bf16, f32, dma = jnp.bfloat16, jnp.float32, pltpu.SemaphoreType.DMA
    return pl.pallas_call(
        kernel,
        name="window_attention",
        out_shape=jax.ShapeDtypeStruct((TOK, HEADS * HD), f32),
        in_specs=[pl.BlockSpec(memory_space=pl.ANY)] * 3 + [vmem] * 4,
        out_specs=vmem,
        scratch_shapes=[
            pltpu.VMEM((TOK, HEADS * HD), f32),
            pltpu.VMEM((TOK, HEADS * HD), f32),
            pltpu.VMEM((TOK, HEADS * HD), bf16),
            pltpu.VMEM((SLOTS, HD, TOK), bf16),
            pltpu.VMEM((SLOTS, TOK, HD), bf16),
            pltpu.VMEM((8, HD, TOK), bf16),
            pltpu.VMEM((4, 2, 128), jnp.int32),
            pltpu.VMEM((HEADS, HD, TOK), bf16),
            pltpu.VMEM((HEADS, TOK, HD), bf16),
            pltpu.VMEM((HEADS, HD, TOK), bf16),
            pltpu.VMEM((8, 128), f32),
            pltpu.VMEM((TENSOR, 8, 128), f32),
            pltpu.VMEM((8, 128), f32),
            pltpu.SMEM((8, 128), f32),
            pltpu.VMEM((8, 1, TOK), f32),
            pltpu.VMEM((8, 1, TOK), f32),
            pltpu.VMEM((8, HD, TOK), f32),
            pltpu.VMEM((4, TOK, HD), bf16),
            pltpu.VMEM((4, TOK, HD), bf16),
            pltpu.VMEM((4, HD, TOK), bf16),
            pltpu.VMEM((4, HD, TOK), bf16),
            pltpu.VMEM((4, 2, TOK), f32),
            pltpu.VMEM((4, 2, TOK), f32),
            dma((128,)),
            dma,
            dma((3,)),
            dma((2, SLOTS)),
            dma((8,)),
            dma((4,)),
            dma((TENSOR,)),
            dma((4,)),
            dma((4,)),
            dma((4,)),
        ],
        compiler_params=pltpu.CompilerParams(collective_id=0, has_side_effects=True),
    )(q_in, k_in, v_in, q_gain, k_gain, adjacent, frames)


def solution(mesh):
    return jax.shard_map(
        shards,
        mesh=mesh,
        in_specs=(
            P("seq", "tensor"),
            P("seq", "tensor"),
            P("seq", "tensor"),
            P("tensor"),
            P("tensor"),
            P(),
            P("seq", None),
        ),
        out_specs=P("seq", "tensor"),
        check_vma=False,
    )
```

```python
import math

import jax
import jax.numpy as jnp
from jax import lax
from jax.experimental import pallas as pl
from jax.experimental.pallas import tpu as pltpu
from jax.sharding import PartitionSpec as P

HD = 128
TOK = 256
HEADS = 5
CHIPS = 4
PLANES = 8
TENSOR = 8
SLOTS = 36
COLUMN = 28
MESH = pl.DeviceIdType.MESH
EPS = 1e-06
BLOCKED = -1e30
EXP2_SCALE = math.log2(math.e) / math.sqrt(HD)


def place():
    s = lax.axis_index("seq")
    return lax.div(s, 8), lax.rem(lax.div(s, 2), 4), lax.rem(s, 2), lax.axis_index("tensor")


def fold(tiles, m_sc, l_sc, acc_sc):
    halves = (slice(0, 128), slice(128, 256))
    count = len(tiles)
    scores, weights, fades, sums = {}, {}, {}, {}

    def score(n):
        state, queries, keys, values, bias = tiles[n]
        scores[n] = jnp.dot(keys, queries, preferred_element_type=jnp.float32)

    def weigh(n):
        state, queries, keys, values, bias = tiles[n]
        s = scores.pop(n)
        blocks = s.shape[0] // 128
        columns, news, totals = [], [], []
        for a in range(2):
            new = m_sc[state, :, halves[a]]
            for b in range(blocks):
                top = jnp.max(s[b * 128 : (b + 1) * 128, halves[a]], axis=0, keepdims=True)
                new = jnp.maximum(new, top * EXP2_SCALE + bias[a][b])
            parts = [
                jnp.exp2(s[b * 128 : (b + 1) * 128, halves[a]] * EXP2_SCALE - (new - bias[a][b]))
                for b in range(blocks)
            ]
            column = jnp.concatenate(parts, axis=0)
            totals.append(jnp.sum(column, axis=0, keepdims=True))
            columns.append(column.astype(jnp.bfloat16))
            news.append(new)
        new = jnp.concatenate(news, axis=1)
        fades[n] = jnp.exp2(m_sc[state] - new)
        m_sc[state] = new
        l_sc[state] = l_sc[state] * fades[n] + jnp.concatenate(totals, axis=1)
        weights[n] = jnp.concatenate(columns, axis=1)

    def mix(n):
        state, queries, keys, values, bias = tiles[n]
        mixed = jnp.dot(values, weights.pop(n), preferred_element_type=jnp.float32)
        acc_sc[state] = acc_sc[state] * fades.pop(n) + mixed

    score(0)
    for n in range(count):
        if n + 1 < count:
            score(n + 1)
        if n > 0:
            mix(n - 1)
        weigh(n)
    mix(count - 1)


def kernel(
    q_hbm, k_hbm, v_hbm, qg_ref, kg_ref, adj_ref, frames_ref,
    out_ref,
    q_ref, k_ref, v_ref,
    vs, ks, qs, adju, qn, kn, vt, stat, statr,
    bias_v, bias_s, m_sc, l_sc, acc_sc, obuf, rbuf, obuf4, rbuf4, ost, rst,
    ssem, bsem, isem, rkv, rq, ra, rstat, ro, ro4, rost,
):
    z, h, k, t = place()
    other = 1 - k
    kv = (vs, ks)
    s_me = lax.axis_index("seq")
    upper = lax.div(h, 2)
    far_core = 1 - upper
    is_far = k == far_core

    def dev(zz, hh, kk):
        return (lax.rem(zz + PLANES, PLANES) * 8 + hh * 2 + kk, t)

    def chip(step):
        return lax.rem(h + step, CHIPS)

    sends = []

    def send(src, dst, rsem, device, condition=None):
        copy = pltpu.make_async_remote_copy(
            src_ref=src, dst_ref=dst, send_sem=ssem.at[len(sends)], recv_sem=rsem,
            device_id=device, device_id_type=MESH,
        )
        sends.append((copy, condition))
        if condition is None:
            copy.start()
        else:
            pl.when(condition)(copy.start)

    def send_kv(v, src, slot, device):
        send(src, kv[v].at[slot], rkv.at[v, slot], device)

    def arrived(dst, rsem):
        pltpu.make_async_copy(dst, dst, rsem).wait()

    def arrived_kv(v, slot):
        arrived(kv[v].at[slot], rkv.at[v, slot])

    loads = [
        pltpu.make_async_copy(src, dst, isem.at[n])
        for n, (src, dst) in enumerate(((q_hbm, q_ref), (k_hbm, k_ref), (v_hbm, v_ref)))
    ]
    for load in loads:
        load.start()

    barrier = pltpu.get_barrier_semaphore()
    peers = [dev(z, h, other)]
    for step in (1, 2, 3):
        peers += [dev(z, chip(step), 0), dev(z, chip(step), 1)]
    for zz in (z + 1, z - 1):
        peers += [dev(zz, h, 0), dev(zz, h, 1)]
    for step in range(1, TENSOR):
        peers.append((s_me, lax.rem(t + step, TENSOR)))
    for peer in peers:
        pl.semaphore_signal(barrier, inc=1, device_id=peer, device_id_type=MESH)

    for load in loads:
        load.wait()

    eye = lax.broadcasted_iota(jnp.int32, (128, 128), 0) == lax.broadcasted_iota(
        jnp.int32, (128, 128), 1
    )
    rows = []
    for ref in (q_ref, k_ref):
        for half in range(2):
            part = ref[half * 128 : (half + 1) * 128, :]
            column = jnp.sum(part * part, axis=1, keepdims=True)
            rows.append(jnp.sum(jnp.where(eye, column, 0.0), axis=0, keepdims=True))
    mine = jnp.concatenate(rows + [jnp.zeros((4, 128), jnp.float32)], axis=0)
    stat[...] = mine
    statr[t] = mine

    def u_slot(position, core):
        return position + 12 - 4 * core

    own = 2 * h + k
    for i in range(HEADS):
        vt[i] = v_ref[:, i * HD : (i + 1) * HD].T
    vs[u_slot(own, k)] = vt[h]
    vs[COLUMN + 2 + k] = vt[4]
    m_sc[...] = jnp.full_like(m_sc, -1e29)
    l_sc[...] = jnp.zeros_like(l_sc)
    acc_sc[...] = jnp.zeros_like(acc_sc)

    pl.semaphore_wait(barrier, len(peers))

    for step in range(1, TENSOR):
        send(stat, statr.at[t], rstat.at[t], (s_me, lax.rem(t + step, TENSOR)))

    def spread_u(v, hp, src):
        p = 2 * hp + k
        send_kv(v, src, u_slot(p - 8, k), dev(z + 1, h, k))
        send_kv(v, src, u_slot(p + 8, k), dev(z - 1, h, k))
        send_kv(v, src, u_slot(p, other), dev(z, h, other))

    def first_y(v, ref, steps):
        for step in steps:
            send_kv(v, ref.at[chip(step)], u_slot(own, k), dev(z, chip(step), k))

    def first_z(v, ref):
        spread_u(v, h, ref.at[h])
        send_kv(v, ref.at[4], COLUMN + k, dev(z + 1, h, k))
        send_kv(v, ref.at[4], COLUMN + 4 + k, dev(z - 1, h, k))
        send_kv(v, ref.at[4], COLUMN + 2 + k, dev(z, h, other))

    first_y(0, vt, (2, 1, 3))
    first_z(0, vt)

    core = upper
    place_q = 2 * lax.rem(h, 2) + k
    to_self = core == k
    to_other = jnp.logical_not(to_self)
    for step in (1, 2, 3):
        send(adj_ref, adju.at[place_q], ra.at[place_q], dev(z, chip(step), core))
    send(adj_ref, adju.at[place_q], ra.at[place_q], dev(z, h, other), to_other)

    for step in range(1, TENSOR):
        j = lax.rem(t + step, TENSOR)
        arrived(statr.at[j], rstat.at[j])
    total = statr[0]
    for j in range(1, TENSOR):
        total = total + statr[j]
    inverse = 1.0 / jnp.sqrt(total / float(HD * HEADS * TENSOR) + EPS)

    def normalize(row, half, ref, gain, put):
        lane_row = inverse[row + half : row + half + 1, :]
        column = jnp.sum(jnp.where(eye, lane_row, 0.0), axis=1, keepdims=True)
        span = slice(half * 128, (half + 1) * 128)
        for i in range(HEADS):
            feature = slice(i * HD, (i + 1) * HD)
            put(i, span, ref[span, feature] * column * gain[feature][None, :])

    def put_k(i, span, x):
        kn[i, span, :] = x.astype(jnp.bfloat16)

    def put_q(i, span, x):
        qn[i, :, span] = x.T.astype(jnp.bfloat16)

    normalize(2, 0, k_ref, kg_ref, put_k)
    normalize(2, 1, k_ref, kg_ref, put_k)
    normalize(0, 0, q_ref, qg_ref, put_q)
    first_z(1, kn)
    ks[u_slot(own, k)] = kn[h]
    ks[COLUMN + 2 + k] = kn[4]
    normalize(0, 1, q_ref, qg_ref, put_q)

    @pl.when(to_self)
    def _():
        qs[place_q] = qn[h]
        qs[4 + place_q] = qn[4]
        adju[place_q] = adj_ref[...]

    for base, head in ((0, chip), (4, lambda step: 4)):
        at = base + place_q
        for step in (2, 1, 3):
            send(qn.at[head(step)], qs.at[at], rq.at[at], dev(z, chip(step), core))
        send(qn.at[head(0)], qs.at[at], rq.at[at], dev(z, h, other), to_other)
    first_y(1, kn, (1, 3, 2))

    def plane_u(v, step):
        slot = u_slot(2 * chip(step) + k, k)
        arrived_kv(v, slot)
        spread_u(v, chip(step), kv[v].at[slot])

    def planes_u(v, step):
        hp = chip(step)
        sign = 1 - 2 * lax.div(hp, 2)
        p = 2 * hp + k
        for q in (p - 8, p + 8):
            arrived_kv(v, u_slot(q, k))
        far = lax.div(1 + sign, 2)
        send_kv(
            v, kv[v].at[u_slot(p + 8 * sign, k)], u_slot(p + 16 * sign, far),
            dev(z - sign, h, far),
        )
        for q in (p - 8, p + 8):
            send_kv(v, kv[v].at[u_slot(q, k)], u_slot(q, other), dev(z, h, other))

    def planes_4(v):
        low, high = COLUMN + k, COLUMN + 4 + k
        arrived_kv(v, low)
        arrived_kv(v, high)
        send_kv(
            v, kv[v].at[COLUMN + 4 * far_core + k], COLUMN + 6 + k,
            dev(z + 2 * upper - 1, h, far_core),
        )
        for slot in (low, high):
            send_kv(v, kv[v].at[slot], slot, dev(z, h, other))

    def mine_q(i):
        return jnp.logical_and(to_self, place_q == i)

    def unless_mine(i, wait):
        pl.when(jnp.logical_not(mine_q(i)))(wait)

    def biases_ready():
        frame_row = frames_ref[...][None, :]
        lane = lax.broadcasted_iota(jnp.int32, (1, 128), 1)
        rows = []
        for i in range(4):
            unless_mine(i, lambda: arrived(adju.at[i], ra.at[i]))
            shard = 8 * z + 4 * k + i
            for a in range(2):
                at = jnp.where(lane == 2 * shard + a, frame_row, -1)
                gap = jnp.abs(frame_row - jnp.max(at, axis=1, keepdims=True))
                fine = (gap == 0) | ((gap == 1) & (adju[i, a : a + 1, :] == 1))
                rows.append(jnp.where(fine, 0.0, BLOCKED))
        bias_v[...] = jnp.concatenate(rows, axis=0)

    def bias_copy():
        return pltpu.make_async_copy(bias_v, bias_s, bsem)

    def bias_of(i, first_shard):
        found = [[], []]
        for shard in (first_shard, first_shard + 1):
            valid = jnp.logical_and(shard >= 0, shard < 64)
            at = jnp.clip(shard, 0, 63)
            for a in range(2):
                for b in range(2):
                    found[a].append(jnp.where(valid, bias_s[2 * i + a, 2 * at + b], BLOCKED))
        return found

    def keys_of(n):
        step = jnp.where(
            n < 3, 0, jnp.where(n < 5, 2 * n - 5, jnp.where(n < 7, 1, jnp.where(n < 9, 3, 2)))
        )
        turn = jnp.where(
            n < 3, n, jnp.where(n < 5, 0, jnp.where(n < 7, n - 4, jnp.where(n < 9, n - 6, n - 9)))
        )
        dz = jnp.where(turn == 0, 0, 2 * turn - 3)
        slot = jnp.where(
            n >= 12, 24 * k + 2 * (n - 12), u_slot(8 * dz + 2 * lax.rem(h + step, CHIPS), k)
        )
        shard = 8 * z + 4 * k + slot - 12
        turn4 = n - 14
        dz4 = jnp.where(turn4 == 3, 2 - 4 * upper, jnp.where(turn4 == 0, 0, 2 * turn4 - 3))
        slot4 = COLUMN + jnp.where(turn4 == 0, 2, jnp.where(turn4 == 1, 0, 2 * turn4))
        column = n >= 14
        slot = jnp.where(column, slot4, slot)
        shard = jnp.where(column, 8 * (z + dz4) + 2 * h, shard)
        keys = ks[pl.ds(slot, 2)].reshape(2 * TOK, HD)
        values = jnp.concatenate([vs[slot], vs[slot + 1]], axis=1)
        return keys, values, shard, jnp.where(column, 4, 0)

    def unit(n, carry):
        keys, values, shard, base = keys_of(n)
        fold(
            [(base + i, qs[base + i], keys, values, bias_of(i, shard)) for i in range(4)],
            m_sc, l_sc, acc_sc,
        )
        return carry

    def last_units(low):
        def pair(j, carry):
            tiles = []
            for n in (10 + 2 * j, 11 + 2 * j):
                keys, values, shard, _ = keys_of(n)
                for i in (low, low + 1):
                    tiles.append((i, qs[i], keys, values, bias_of(i, shard)))
            fold(tiles, m_sc, l_sc, acc_sc)
            return carry

        lax.fori_loop(0, 2, pair, 0)

    def from_partner(dz, step):
        for v in range(2):
            arrived_kv(v, u_slot(8 * dz + 2 * chip(step) + other, k))

    def compute(begin, end):
        lax.fori_loop(begin, end, unit, 0)

    def owner(i):
        return 2 * k + i // 2, i % 2

    def away(i):
        hh, kk = owner(i)
        return jnp.logical_not(jnp.logical_and(hh == h, kk == k))

    def give(i, src, dst, rsem):
        send(src.at[i], dst.at[h], rsem.at[h], dev(z, *owner(i)), away(i))

        @pl.when(jnp.logical_not(away(i)))
        def _():
            dst[h] = src[i]

    planes_u(0, 0)
    planes_4(0)
    plane_u(0, 1)
    plane_u(0, 3)
    plane_u(0, 2)
    biases_ready()
    planes_u(1, 0)
    planes_4(1)
    planes_u(0, 1)
    planes_u(0, 3)
    bias_copy().start()
    planes_u(0, 2)
    bias_copy().wait()
    for i in range(4):
        unless_mine(i, lambda: arrived(qs.at[i], rq.at[i]))
    for dz in (0, -1, 1):
        from_partner(dz, 0)
    compute(0, 3)

    for i in range(4):
        unless_mine(i, lambda: arrived(qs.at[4 + i], rq.at[4 + i]))
    for v in range(2):
        for slot in (0, 2, 4):
            arrived_kv(v, COLUMN + slot + other)

        @pl.when(is_far)
        def _():
            arrived_kv(v, COLUMN + 6)
            arrived_kv(v, COLUMN + 7)

    compute(14, 16)
    plane_u(1, 1)
    plane_u(1, 3)
    compute(16, jnp.where(is_far, 18, 17))
    for i in range(4):
        total = l_sc[4 + i]
        obuf4[i] = (acc_sc[4 + i] / jnp.maximum(total, 1e-30)).astype(jnp.bfloat16)
        ost[i] = jnp.concatenate([m_sc[4 + i], total], axis=0)
    plane_u(1, 2)
    for i in range(4):
        give(i, obuf4, rbuf4, ro4)
        give(i, ost, rst, rost)
    planes_u(1, 1)
    planes_u(1, 3)
    for step in (1, 3):
        from_partner(0, step)
    compute(3, 5)
    planes_u(1, 2)
    for step in (1, 3):
        from_partner(-1, step)
        from_partner(1, step)
    compute(5, 9)
    from_partner(0, 2)
    from_partner(-1, 2)
    from_partner(1, 2)
    for v in range(2):
        for i in range(4):
            arrived_kv(v, 24 * k + i)
    compute(9, 10)

    gathered = len(sends)

    for low in (0, 2):
        last_units(low)
        for i in (low, low + 1):
            obuf[i] = (acc_sc[i] / l_sc[i]).T.astype(jnp.bfloat16)
        for i in (low, low + 1):
            give(i, obuf, rbuf, ro)

    def all_left(begin, end):
        for copy, condition in sends[begin:end]:
            if condition is None:
                copy.wait_send()
            else:
                pl.when(condition)(copy.wait_send)

    def returned(head, dst, rsem):
        pl.when(jnp.logical_not(jnp.logical_and(to_self, head == h)))(
            lambda: arrived(dst.at[head], rsem.at[head])
        )

    for head in range(4):
        returned(head, rbuf4, ro4)
        returned(head, rst, rost)
    top = jnp.maximum(
        jnp.maximum(rst[0, 0:1], rst[1, 0:1]), jnp.maximum(rst[2, 0:1], rst[3, 0:1])
    )
    shares = [rst[j, 1:2] * jnp.exp2(rst[j, 0:1] - top) for j in range(4)]
    whole = shares[0] + shares[1] + shares[2] + shares[3]
    merged = rbuf4[0].astype(jnp.float32) * shares[0]
    for j in range(1, 4):
        merged = merged + rbuf4[j].astype(jnp.float32) * shares[j]
    out_ref[:, 4 * HD :] = (merged / whole).T
    all_left(0, gathered)
    for head in range(4):
        returned(head, rbuf, ro)
    for head in range(4):
        out_ref[:, head * HD : (head + 1) * HD] = rbuf[head].astype(jnp.float32)

    all_left(gathered, len(sends))


def shards(q_in, k_in, v_in, q_gain, k_gain, frames, adjacent):
    vmem = pl.BlockSpec(memory_space=pltpu.VMEM)
    bf16, f32, dma = jnp.bfloat16, jnp.float32, pltpu.SemaphoreType.DMA
    return pl.pallas_call(
        kernel,
        name="window_attention",
        out_shape=jax.ShapeDtypeStruct((TOK, HEADS * HD), f32),
        in_specs=[pl.BlockSpec(memory_space=pl.ANY)] * 3 + [vmem] * 4,
        out_specs=vmem,
        scratch_shapes=[
            pltpu.VMEM((TOK, HEADS * HD), f32),
            pltpu.VMEM((TOK, HEADS * HD), f32),
            pltpu.VMEM((TOK, HEADS * HD), bf16),
            pltpu.VMEM((SLOTS, HD, TOK), bf16),
            pltpu.VMEM((SLOTS, TOK, HD), bf16),
            pltpu.VMEM((8, HD, TOK), bf16),
            pltpu.VMEM((4, 2, 128), jnp.int32),
            pltpu.VMEM((HEADS, HD, TOK), bf16),
            pltpu.VMEM((HEADS, TOK, HD), bf16),
            pltpu.VMEM((HEADS, HD, TOK), bf16),
            pltpu.VMEM((8, 128), f32),
            pltpu.VMEM((TENSOR, 8, 128), f32),
            pltpu.VMEM((8, 128), f32),
            pltpu.SMEM((8, 128), f32),
            pltpu.VMEM((8, 1, TOK), f32),
            pltpu.VMEM((8, 1, TOK), f32),
            pltpu.VMEM((8, HD, TOK), f32),
            pltpu.VMEM((4, TOK, HD), bf16),
            pltpu.VMEM((4, TOK, HD), bf16),
            pltpu.VMEM((4, HD, TOK), bf16),
            pltpu.VMEM((4, HD, TOK), bf16),
            pltpu.VMEM((4, 2, TOK), f32),
            pltpu.VMEM((4, 2, TOK), f32),
            dma((128,)),
            dma,
            dma((3,)),
            dma((2, SLOTS)),
            dma((8,)),
            dma((4,)),
            dma((TENSOR,)),
            dma((4,)),
            dma((4,)),
            dma((4,)),
        ],
        compiler_params=pltpu.CompilerParams(collective_id=0, has_side_effects=True),
    )(q_in, k_in, v_in, q_gain, k_gain, adjacent, frames)


def solution(mesh):
    return jax.shard_map(
        shards,
        mesh=mesh,
        in_specs=(
            P("seq", "tensor"),
            P("seq", "tensor"),
            P("seq", "tensor"),
            P("tensor"),
            P("tensor"),
            P(),
            P("seq", None),
        ),
        out_specs=P("seq", "tensor"),
        check_vma=False,
    )
```

```python
import math

import jax
import jax.numpy as jnp
from jax import lax
from jax.experimental import pallas as pl
from jax.experimental.pallas import tpu as pltpu
from jax.sharding import PartitionSpec as P

HD = 128
TOK = 256
HEADS = 5
CHIPS = 4
PLANES = 8
TENSOR = 8
SLOTS = 36
COLUMN = 28
MESH = pl.DeviceIdType.MESH
EPS = 1e-06
BLOCKED = -1e30
EXP2_SCALE = math.log2(math.e) / math.sqrt(HD)


def place():
    s = lax.axis_index("seq")
    return lax.div(s, 8), lax.rem(lax.div(s, 2), 4), lax.rem(s, 2), lax.axis_index("tensor")


def fold(tiles, m_sc, l_sc, acc_sc):
    halves = (slice(0, 128), slice(128, 256))
    count = len(tiles)
    scores, weights, fades, sums = {}, {}, {}, {}

    def score(n):
        state, queries, keys, values, bias = tiles[n]
        scores[n] = jnp.dot(keys, queries, preferred_element_type=jnp.float32)

    def weigh(n):
        state, queries, keys, values, bias = tiles[n]
        s = scores.pop(n)
        blocks = s.shape[0] // 128
        columns, news, totals = [], [], []
        for a in range(2):
            new = m_sc[state, :, halves[a]]
            for b in range(blocks):
                top = jnp.max(s[b * 128 : (b + 1) * 128, halves[a]], axis=0, keepdims=True)
                new = jnp.maximum(new, top * EXP2_SCALE + bias[a][b])
            parts = [
                jnp.exp2(s[b * 128 : (b + 1) * 128, halves[a]] * EXP2_SCALE - (new - bias[a][b]))
                for b in range(blocks)
            ]
            column = jnp.concatenate(parts, axis=0)
            totals.append(jnp.sum(column, axis=0, keepdims=True))
            columns.append(column.astype(jnp.bfloat16))
            news.append(new)
        new = jnp.concatenate(news, axis=1)
        fades[n] = jnp.exp2(m_sc[state] - new)
        m_sc[state] = new
        l_sc[state] = l_sc[state] * fades[n] + jnp.concatenate(totals, axis=1)
        weights[n] = jnp.concatenate(columns, axis=1)

    def mix(n):
        state, queries, keys, values, bias = tiles[n]
        mixed = jnp.dot(values, weights.pop(n), preferred_element_type=jnp.float32)
        acc_sc[state] = acc_sc[state] * fades.pop(n) + mixed

    score(0)
    for n in range(count):
        if n + 1 < count:
            score(n + 1)
        if n > 0:
            mix(n - 1)
        weigh(n)
    mix(count - 1)


def kernel(
    q_hbm, k_hbm, v_hbm, qg_ref, kg_ref, adj_ref, frames_ref,
    out_ref,
    q_ref, k_ref, v_ref,
    vs, ks, qs, adju, qn, kn, vt, stat, statr,
    bias_v, bias_s, m_sc, l_sc, acc_sc, obuf, rbuf, obuf4, rbuf4, ost, rst,
    ssem, bsem, isem, rkv, rq, ra, rstat, ro, ro4, rost,
):
    z, h, k, t = place()
    other = 1 - k
    kv = (vs, ks)
    s_me = lax.axis_index("seq")
    upper = lax.div(h, 2)
    far_core = 1 - upper
    is_far = k == far_core

    def dev(zz, hh, kk):
        return (lax.rem(zz + PLANES, PLANES) * 8 + hh * 2 + kk, t)

    def chip(step):
        return lax.rem(h + step, CHIPS)

    sends = []

    def send(src, dst, rsem, device, condition=None):
        copy = pltpu.make_async_remote_copy(
            src_ref=src, dst_ref=dst, send_sem=ssem.at[len(sends)], recv_sem=rsem,
            device_id=device, device_id_type=MESH,
        )
        sends.append((copy, condition))
        if condition is None:
            copy.start()
        else:
            pl.when(condition)(copy.start)

    def send_kv(v, src, slot, device):
        send(src, kv[v].at[slot], rkv.at[v, slot], device)

    def arrived(dst, rsem):
        pltpu.make_async_copy(dst, dst, rsem).wait()

    def arrived_kv(v, slot):
        arrived(kv[v].at[slot], rkv.at[v, slot])

    loads = [
        pltpu.make_async_copy(src, dst, isem.at[n])
        for n, (src, dst) in enumerate(((q_hbm, q_ref), (k_hbm, k_ref), (v_hbm, v_ref)))
    ]
    for load in loads:
        load.start()

    barrier = pltpu.get_barrier_semaphore()
    peers = [dev(z, h, other)]
    for step in (1, 2, 3):
        peers += [dev(z, chip(step), 0), dev(z, chip(step), 1)]
    for zz in (z + 1, z - 1):
        peers += [dev(zz, h, 0), dev(zz, h, 1)]
    for step in range(1, TENSOR):
        peers.append((s_me, lax.rem(t + step, TENSOR)))
    for peer in peers:
        pl.semaphore_signal(barrier, inc=1, device_id=peer, device_id_type=MESH)

    for load in loads:
        load.wait()

    eye = lax.broadcasted_iota(jnp.int32, (128, 128), 0) == lax.broadcasted_iota(
        jnp.int32, (128, 128), 1
    )
    rows = []
    for ref in (q_ref, k_ref):
        for half in range(2):
            part = ref[half * 128 : (half + 1) * 128, :]
            column = jnp.sum(part * part, axis=1, keepdims=True)
            rows.append(jnp.sum(jnp.where(eye, column, 0.0), axis=0, keepdims=True))
    mine = jnp.concatenate(rows + [jnp.zeros((4, 128), jnp.float32)], axis=0)
    stat[...] = mine
    statr[t] = mine

    def u_slot(position, core):
        return position + 12 - 4 * core

    own = 2 * h + k
    for i in range(HEADS):
        vt[i] = v_ref[:, i * HD : (i + 1) * HD].T
    vs[u_slot(own, k)] = vt[h]
    vs[COLUMN + 2 + k] = vt[4]
    m_sc[...] = jnp.full_like(m_sc, -1e29)
    l_sc[...] = jnp.zeros_like(l_sc)
    acc_sc[...] = jnp.zeros_like(acc_sc)

    pl.semaphore_wait(barrier, len(peers))

    for step in range(1, TENSOR):
        send(stat, statr.at[t], rstat.at[t], (s_me, lax.rem(t + step, TENSOR)))

    def spread_u(v, hp, src):
        p = 2 * hp + k
        send_kv(v, src, u_slot(p - 8, k), dev(z + 1, h, k))
        send_kv(v, src, u_slot(p + 8, k), dev(z - 1, h, k))
        send_kv(v, src, u_slot(p, other), dev(z, h, other))

    def first_y(v, ref, steps):
        for step in steps:
            send_kv(v, ref.at[chip(step)], u_slot(own, k), dev(z, chip(step), k))

    def first_z(v, ref):
        spread_u(v, h, ref.at[h])
        send_kv(v, ref.at[4], COLUMN + k, dev(z + 1, h, k))
        send_kv(v, ref.at[4], COLUMN + 4 + k, dev(z - 1, h, k))
        send_kv(v, ref.at[4], COLUMN + 2 + k, dev(z, h, other))

    first_y(0, vt, (2, 1, 3))
    first_z(0, vt)

    core = upper
    place_q = 2 * lax.rem(h, 2) + k
    to_self = core == k
    to_other = jnp.logical_not(to_self)
    for step in (1, 2, 3):
        send(adj_ref, adju.at[place_q], ra.at[place_q], dev(z, chip(step), core))
    send(adj_ref, adju.at[place_q], ra.at[place_q], dev(z, h, other), to_other)

    for step in range(1, TENSOR):
        j = lax.rem(t + step, TENSOR)
        arrived(statr.at[j], rstat.at[j])
    total = statr[0]
    for j in range(1, TENSOR):
        total = total + statr[j]
    inverse = 1.0 / jnp.sqrt(total / float(HD * HEADS * TENSOR) + EPS)

    def normalize(row, half, ref, gain, put):
        lane_row = inverse[row + half : row + half + 1, :]
        column = jnp.sum(jnp.where(eye, lane_row, 0.0), axis=1, keepdims=True)
        span = slice(half * 128, (half + 1) * 128)
        for i in range(HEADS):
            feature = slice(i * HD, (i + 1) * HD)
            put(i, span, ref[span, feature] * column * gain[feature][None, :])

    def put_k(i, span, x):
        kn[i, span, :] = x.astype(jnp.bfloat16)

    def put_q(i, span, x):
        qn[i, :, span] = x.T.astype(jnp.bfloat16)

    normalize(2, 0, k_ref, kg_ref, put_k)
    normalize(2, 1, k_ref, kg_ref, put_k)
    normalize(0, 0, q_ref, qg_ref, put_q)
    first_z(1, kn)
    ks[u_slot(own, k)] = kn[h]
    ks[COLUMN + 2 + k] = kn[4]
    normalize(0, 1, q_ref, qg_ref, put_q)

    @pl.when(to_self)
    def _():
        qs[place_q] = qn[h]
        qs[4 + place_q] = qn[4]
        adju[place_q] = adj_ref[...]

    for base, head in ((0, chip), (4, lambda step: 4)):
        at = base + place_q
        for step in (2, 1, 3):
            send(qn.at[head(step)], qs.at[at], rq.at[at], dev(z, chip(step), core))
        send(qn.at[head(0)], qs.at[at], rq.at[at], dev(z, h, other), to_other)
    first_y(1, kn, (1, 3, 2))

    def plane_u(v, step):
        slot = u_slot(2 * chip(step) + k, k)
        arrived_kv(v, slot)
        spread_u(v, chip(step), kv[v].at[slot])

    def planes_u(v, step):
        hp = chip(step)
        sign = 1 - 2 * lax.div(hp, 2)
        p = 2 * hp + k
        for q in (p - 8, p + 8):
            arrived_kv(v, u_slot(q, k))
        far = lax.div(1 + sign, 2)
        send_kv(
            v, kv[v].at[u_slot(p + 8 * sign, k)], u_slot(p + 16 * sign, far),
            dev(z - sign, h, far),
        )
        for q in (p - 8, p + 8):
            send_kv(v, kv[v].at[u_slot(q, k)], u_slot(q, other), dev(z, h, other))

    def planes_4(v):
        low, high = COLUMN + k, COLUMN + 4 + k
        arrived_kv(v, low)
        arrived_kv(v, high)
        send_kv(
            v, kv[v].at[COLUMN + 4 * far_core + k], COLUMN + 6 + k,
            dev(z + 2 * upper - 1, h, far_core),
        )
        for slot in (low, high):
            send_kv(v, kv[v].at[slot], slot, dev(z, h, other))

    def mine_q(i):
        return jnp.logical_and(to_self, place_q == i)

    def unless_mine(i, wait):
        pl.when(jnp.logical_not(mine_q(i)))(wait)

    def biases_ready():
        frame_row = frames_ref[...][None, :]
        lane = lax.broadcasted_iota(jnp.int32, (1, 128), 1)
        rows = []
        for i in range(4):
            unless_mine(i, lambda: arrived(adju.at[i], ra.at[i]))
            shard = 8 * z + 4 * k + i
            for a in range(2):
                at = jnp.where(lane == 2 * shard + a, frame_row, -1)
                gap = jnp.abs(frame_row - jnp.max(at, axis=1, keepdims=True))
                fine = (gap == 0) | ((gap == 1) & (adju[i, a : a + 1, :] == 1))
                rows.append(jnp.where(fine, 0.0, BLOCKED))
        bias_v[...] = jnp.concatenate(rows, axis=0)

    def bias_copy():
        return pltpu.make_async_copy(bias_v, bias_s, bsem)

    def bias_of(i, first_shard):
        found = [[], []]
        for shard in (first_shard, first_shard + 1):
            valid = jnp.logical_and(shard >= 0, shard < 64)
            at = jnp.clip(shard, 0, 63)
            for a in range(2):
                for b in range(2):
                    found[a].append(jnp.where(valid, bias_s[2 * i + a, 2 * at + b], BLOCKED))
        return found

    def keys_of(n):
        step = jnp.where(
            n < 3, 0, jnp.where(n < 5, 2 * n - 5, jnp.where(n < 7, 1, jnp.where(n < 9, 3, 2)))
        )
        turn = jnp.where(
            n < 3, n, jnp.where(n < 5, 0, jnp.where(n < 7, n - 4, jnp.where(n < 9, n - 6, n - 9)))
        )
        dz = jnp.where(turn == 0, 0, 2 * turn - 3)
        slot = jnp.where(
            n >= 12, 24 * k + 2 * (n - 12), u_slot(8 * dz + 2 * lax.rem(h + step, CHIPS), k)
        )
        shard = 8 * z + 4 * k + slot - 12
        turn4 = n - 14
        dz4 = jnp.where(turn4 == 3, 2 - 4 * upper, jnp.where(turn4 == 0, 0, 2 * turn4 - 3))
        slot4 = COLUMN + jnp.where(turn4 == 0, 2, jnp.where(turn4 == 1, 0, 2 * turn4))
        column = n >= 14
        slot = jnp.where(column, slot4, slot)
        shard = jnp.where(column, 8 * (z + dz4) + 2 * h, shard)
        keys = ks[pl.ds(slot, 2)].reshape(2 * TOK, HD)
        values = jnp.concatenate([vs[slot], vs[slot + 1]], axis=1)
        return keys, values, shard, jnp.where(column, 4, 0)

    def unit(n, carry):
        keys, values, shard, base = keys_of(n)
        fold(
            [(base + i, qs[base + i], keys, values, bias_of(i, shard)) for i in range(4)],
            m_sc, l_sc, acc_sc,
        )
        return carry

    def far_planes():
        for v in range(2):
            for i in range(4):
                arrived_kv(v, 24 * k + i)

    def last_units(low):
        def pair(j, carry):
            if low == 0:
                pl.when(j == 1)(far_planes)
            tiles = []
            for n in (10 + 2 * j, 11 + 2 * j):
                keys, values, shard, _ = keys_of(n)
                for i in (low, low + 1):
                    tiles.append((i, qs[i], keys, values, bias_of(i, shard)))
            fold(tiles, m_sc, l_sc, acc_sc)
            return carry

        lax.fori_loop(0, 2, pair, 0)

    def from_partner(dz, step):
        for v in range(2):
            arrived_kv(v, u_slot(8 * dz + 2 * chip(step) + other, k))

    def compute(begin, end):
        lax.fori_loop(begin, end, unit, 0)

    def owner(i):
        return 2 * k + i // 2, i % 2

    def away(i):
        hh, kk = owner(i)
        return jnp.logical_not(jnp.logical_and(hh == h, kk == k))

    def give(i, src, dst, rsem):
        send(src.at[i], dst.at[h], rsem.at[h], dev(z, *owner(i)), away(i))

        @pl.when(jnp.logical_not(away(i)))
        def _():
            dst[h] = src[i]

    planes_u(0, 0)
    planes_4(0)
    plane_u(0, 1)
    plane_u(0, 3)
    plane_u(0, 2)
    biases_ready()
    planes_u(1, 0)
    planes_4(1)
    planes_u(0, 1)
    planes_u(0, 3)
    bias_copy().start()
    planes_u(0, 2)
    bias_copy().wait()
    for i in range(4):
        unless_mine(i, lambda: arrived(qs.at[i], rq.at[i]))
    for dz in (0, -1, 1):
        from_partner(dz, 0)
    compute(0, 3)

    for i in range(4):
        unless_mine(i, lambda: arrived(qs.at[4 + i], rq.at[4 + i]))
    for v in range(2):
        for slot in (0, 2, 4):
            arrived_kv(v, COLUMN + slot + other)

        @pl.when(is_far)
        def _():
            arrived_kv(v, COLUMN + 6)
            arrived_kv(v, COLUMN + 7)

    compute(14, 16)
    plane_u(1, 1)
    plane_u(1, 3)
    compute(16, jnp.where(is_far, 18, 17))
    for i in range(4):
        total = l_sc[4 + i]
        obuf4[i] = (acc_sc[4 + i] / jnp.maximum(total, 1e-30)).astype(jnp.bfloat16)
        ost[i] = jnp.concatenate([m_sc[4 + i], total], axis=0)
    plane_u(1, 2)
    for i in range(4):
        give(i, obuf4, rbuf4, ro4)
        give(i, ost, rst, rost)
    planes_u(1, 1)
    planes_u(1, 3)
    for step in (1, 3):
        from_partner(0, step)
    compute(3, 5)
    planes_u(1, 2)
    for step in (1, 3):
        from_partner(-1, step)
        from_partner(1, step)
    compute(5, 9)
    from_partner(0, 2)
    compute(9, 10)
    from_partner(-1, 2)
    from_partner(1, 2)

    gathered = len(sends)

    for low in (0, 2):
        last_units(low)
        for i in (low, low + 1):
            obuf[i] = (acc_sc[i] / l_sc[i]).T.astype(jnp.bfloat16)
        for i in (low, low + 1):
            give(i, obuf, rbuf, ro)

    def all_left(begin, end):
        for copy, condition in sends[begin:end]:
            if condition is None:
                copy.wait_send()
            else:
                pl.when(condition)(copy.wait_send)

    def returned(head, dst, rsem):
        pl.when(jnp.logical_not(jnp.logical_and(to_self, head == h)))(
            lambda: arrived(dst.at[head], rsem.at[head])
        )

    for head in range(4):
        returned(head, rbuf4, ro4)
        returned(head, rst, rost)
    top = jnp.maximum(
        jnp.maximum(rst[0, 0:1], rst[1, 0:1]), jnp.maximum(rst[2, 0:1], rst[3, 0:1])
    )
    shares = [rst[j, 1:2] * jnp.exp2(rst[j, 0:1] - top) for j in range(4)]
    whole = shares[0] + shares[1] + shares[2] + shares[3]
    merged = rbuf4[0].astype(jnp.float32) * shares[0]
    for j in range(1, 4):
        merged = merged + rbuf4[j].astype(jnp.float32) * shares[j]
    out_ref[:, 4 * HD :] = (merged / whole).T
    all_left(0, gathered)
    for head in range(4):
        returned(head, rbuf, ro)
    for head in range(4):
        out_ref[:, head * HD : (head + 1) * HD] = rbuf[head].astype(jnp.float32)

    all_left(gathered, len(sends))


def shards(q_in, k_in, v_in, q_gain, k_gain, frames, adjacent):
    vmem = pl.BlockSpec(memory_space=pltpu.VMEM)
    bf16, f32, dma = jnp.bfloat16, jnp.float32, pltpu.SemaphoreType.DMA
    return pl.pallas_call(
        kernel,
        name="window_attention",
        out_shape=jax.ShapeDtypeStruct((TOK, HEADS * HD), f32),
        in_specs=[pl.BlockSpec(memory_space=pl.ANY)] * 3 + [vmem] * 4,
        out_specs=vmem,
        scratch_shapes=[
            pltpu.VMEM((TOK, HEADS * HD), f32),
            pltpu.VMEM((TOK, HEADS * HD), f32),
            pltpu.VMEM((TOK, HEADS * HD), bf16),
            pltpu.VMEM((SLOTS, HD, TOK), bf16),
            pltpu.VMEM((SLOTS, TOK, HD), bf16),
            pltpu.VMEM((8, HD, TOK), bf16),
            pltpu.VMEM((4, 2, 128), jnp.int32),
            pltpu.VMEM((HEADS, HD, TOK), bf16),
            pltpu.VMEM((HEADS, TOK, HD), bf16),
            pltpu.VMEM((HEADS, HD, TOK), bf16),
            pltpu.VMEM((8, 128), f32),
            pltpu.VMEM((TENSOR, 8, 128), f32),
            pltpu.VMEM((8, 128), f32),
            pltpu.SMEM((8, 128), f32),
            pltpu.VMEM((8, 1, TOK), f32),
            pltpu.VMEM((8, 1, TOK), f32),
            pltpu.VMEM((8, HD, TOK), f32),
            pltpu.VMEM((4, TOK, HD), bf16),
            pltpu.VMEM((4, TOK, HD), bf16),
            pltpu.VMEM((4, HD, TOK), bf16),
            pltpu.VMEM((4, HD, TOK), bf16),
            pltpu.VMEM((4, 2, TOK), f32),
            pltpu.VMEM((4, 2, TOK), f32),
            dma((128,)),
            dma,
            dma((3,)),
            dma((2, SLOTS)),
            dma((8,)),
            dma((4,)),
            dma((TENSOR,)),
            dma((4,)),
            dma((4,)),
            dma((4,)),
        ],
        compiler_params=pltpu.CompilerParams(collective_id=0, has_side_effects=True),
    )(q_in, k_in, v_in, q_gain, k_gain, adjacent, frames)


def solution(mesh):
    return jax.shard_map(
        shards,
        mesh=mesh,
        in_specs=(
            P("seq", "tensor"),
            P("seq", "tensor"),
            P("seq", "tensor"),
            P("tensor"),
            P("tensor"),
            P(),
            P("seq", None),
        ),
        out_specs=P("seq", "tensor"),
        check_vma=False,
    )
```
